32 devices in a mesh: groups: 2 (over x), ctx: 16 (over z, y, core).
Axes of the slice: x: 2, y: 2, z: 4, core: 2. Of those that a mesh axis runs over, the one named last changes fastest.
Arguments:
- queries: bfloat16 [4096, 8192], P(('groups', 'ctx')), parts along dimension 0, may hold values from -8 to 8
- new_keys: bfloat16 [4096, 1024], P(('groups', 'ctx')), parts along dimension 0, may hold values from -12 to 12
- new_values: bfloat16 [4096, 1024], P(('groups', 'ctx')), parts along dimension 0, may hold values from -6 to 6
- prefix_keys: bfloat16 [256, 1024], P(('groups', 'ctx')), parts along dimension 0, may hold values from -16 to 16
- prefix_values: bfloat16 [256, 1024], P(('groups', 'ctx')), parts along dimension 0, may hold values from -6 to 6
- pool_keys: bfloat16 [32, 2, 256, 1024], P(('groups', 'ctx')), parts along dimension 0, may hold values from -12 to 12
- pool_values: bfloat16 [32, 2, 256, 1024], P(('groups', 'ctx')), parts along dimension 0, may hold values from -6 to 6
- owners: int32 [4], P('groups'), parts along dimension 0, may hold values from 0 to 15
- lengths: int32 [32], P(('groups', 'ctx')), parts along dimension 0, may hold values from 1 to 128, as said below
Outputs:
- attended: bfloat16 [4096, 8192], P(('groups', 'ctx')), parts along dimension 0
The draws below stay inside these ranges and needn't reach their ends.
There are 2 independent parts, one for each index of `groups`. The reference program is written for one: setup_inputs(seed, part) draws one part's arguments, and reference() takes and returns one part's arrays. A program takes and returns all parts, laid end to end along the dimension named above; each array names one. Nothing has to cross between parts.
Inputs may be any that keep to these rules, and one draw needn't show every extreme that they name: `lengths`: some device's prompt fills all 128 slots.
All inputs are finite; a program needn't handle non-finite values.
Results may differ from the reference program's by a relative error of at most 0.0035.
Values may be sent and summed in bfloat16 or wider, within the bound.
A program may use at most 128 MiB of HBM per device.

```python
import jax
import jax.numpy as jnp
from jax import lax

H = 64
KVH = 8
HD = 128
Q_DEV = 128
SB = 2
BLK = 256
PREFIX = 128
TOKENS = 2048
N_CTX = 16


def draw_queries(key, part):
    noise_key = jax.random.fold_in(key, 11)
    values_drawn = jnp.clip(1.5 * jax.random.normal(noise_key, (TOKENS, H * HD), jnp.float32), -8.0, 8.0)
    return values_drawn.astype(jnp.bfloat16)


def draw_prefix_keys(key, part):
    noise_key = jax.random.fold_in(key, 13)
    values_drawn = jnp.clip(2.0 * jax.random.normal(noise_key, (PREFIX, KVH * HD), jnp.float32), -16.0, 16.0)
    return values_drawn.astype(jnp.bfloat16)


def draw_lengths(key, part):
    key_values, key_full = jax.random.split(jax.random.fold_in(key, 23))
    count = TOKENS // Q_DEV
    drawn = jax.random.randint(key_values, (count,), 1, Q_DEV + 1)
    full_index = jax.random.randint(key_full, (), 0, count)
    return drawn.at[full_index].set(Q_DEV).astype(jnp.int32)


def levels(rng, dims, shards, smallest, top_value):
    def one(dim, parts):
        steps = jax.random.uniform(jax.random.fold_in(jax.random.fold_in(rng, 6), dim), (parts,), jnp.float32, smallest / len(shards), top_value / len(shards))
        return jnp.repeat(jnp.exp(steps), dims[dim] // parts).reshape((-1,) + (1,) * (len(dims) - dim - 1))

    gain = one(*shards[0])
    for cut in shards[1:]:
        gain = gain * one(*cut)
    return gain


def centred(own_key, shape, spread, most, cuts=(), kind=jnp.bfloat16):
    entries = spread * jax.random.normal(own_key, shape, jnp.float32)
    if cuts:
        entries = entries * levels(own_key, shape, cuts, -0.22, 0.18)
    return jnp.clip(entries, -most, most).astype(kind)


def setup_inputs(seed: int = 0, part: int = 0) -> dict:
    seeds = jax.random.split(jax.random.key(seed), 10)
    part_splits = jax.random.split(jax.random.fold_in(seeds[9], part), 10)
    return {
        "queries": draw_queries(jax.random.fold_in(jax.random.fold_in(seeds[9], part), 71), part),
        "new_keys": centred(part_splits[1], (TOKENS, KVH * HD), 2.0, 12.0, ((0, 16),)),
        "new_values": centred(part_splits[2], (TOKENS, KVH * HD), 1.0, 6.0, ((0, 16),)),
        "prefix_keys": draw_prefix_keys(jax.random.fold_in(jax.random.fold_in(seeds[9], part), 71), part),
        "prefix_values": centred(part_splits[4], (PREFIX, KVH * HD), 1.0, 6.0, ((0, 16),)),
        "pool_keys": centred(part_splits[5], (N_CTX, SB, BLK, KVH * HD), 2.0, 12.0, ((0, 16),)),
        "pool_values": centred(part_splits[6], (N_CTX, SB, BLK, KVH * HD), 1.0, 6.0, ((0, 16),)),
        "owners": jax.random.randint(part_splits[7], (SB,), 0, N_CTX).astype(jnp.int32),
        "lengths": draw_lengths(jax.random.fold_in(jax.random.fold_in(seeds[9], part), 71), part),
    }


def reference(queries, new_keys, new_values, prefix_keys, prefix_values, pool_keys, pool_values, owners, lengths):
    group_size = H // KVH
    score_scale = 1.0 / (HD ** 0.5)
    block_ids = jnp.arange(SB).astype(jnp.int32)
    shared_keys = pool_keys[owners.astype(jnp.int32), block_ids].reshape(SB * BLK, KVH * HD)
    shared_values = pool_values[owners.astype(jnp.int32), block_ids].reshape(SB * BLK, KVH * HD)

    def one_block(device):
        start = (device * Q_DEV).astype(jnp.int32)
        query_rows = lax.dynamic_slice_in_dim(queries, start, Q_DEV, 0)
        own_keys = lax.dynamic_slice_in_dim(new_keys, start, Q_DEV, 0)
        own_values = lax.dynamic_slice_in_dim(new_values, start, Q_DEV, 0)
        length = lengths[device]
        key_rows = jnp.concatenate([shared_keys, prefix_keys, own_keys], axis=0)
        value_rows = jnp.concatenate([shared_values, prefix_values, own_values], axis=0)
        positions = jnp.arange(Q_DEV).astype(jnp.int32)
        own_visible = (positions[None, :] <= positions[:, None]) & (positions[None, :] < length)
        visible = jnp.concatenate([jnp.ones((Q_DEV, SB * BLK + PREFIX), dtype=bool), own_visible], axis=1)
        visible = jnp.repeat(visible, group_size, axis=0)
        pieces = []
        for kv_head in range(KVH):
            head_queries = query_rows[:, kv_head * group_size * HD:(kv_head + 1) * group_size * HD].reshape(Q_DEV * group_size, HD)
            head_keys = key_rows[:, kv_head * HD:(kv_head + 1) * HD]
            head_values = value_rows[:, kv_head * HD:(kv_head + 1) * HD]
            scores = lax.dot_general(head_queries, head_keys, (((1,), (1,)), ((), ())), preferred_element_type=jnp.float32) * score_scale
            scores = jnp.where(visible, scores, -1e30)
            row_max = jnp.max(scores, axis=1, keepdims=True)
            weights = jnp.where(visible, jnp.exp(scores - row_max), 0.0)
            totals = jnp.sum(weights, axis=1, keepdims=True)
            summed = jnp.dot(weights.astype(jnp.bfloat16), head_values, preferred_element_type=jnp.float32)
            pieces.append((summed / totals).reshape(Q_DEV, group_size * HD))
        joined = jnp.concatenate(pieces, axis=1)
        live = positions < length
        return jnp.where(live[:, None], joined, 0.0).astype(jnp.bfloat16)

    blocks = lax.map(one_block, jnp.arange(TOKENS // Q_DEV).astype(jnp.int32))
    return blocks.reshape(TOKENS, H * HD)
```

```python
import functools

import jax
import jax.numpy as jnp
from jax import lax
from jax.experimental import pallas as pl
from jax.experimental.pallas import tpu as pltpu
from jax.sharding import PartitionSpec as P

HD = 128
CUTS = 1
SIB = 1
HOP = (5, 2)
SUB = 4


def grid_of(ring):
    chips = ring // 2
    short = 1
    while (short * 2) ** 2 <= chips and chips % (short * 2) == 0:
        short *= 2
    return chips // short, short


def kernel(
    ring, heads, kv_heads,
    q_hbm, nk_hbm, nv_hbm, pk_hbm, pv_hbm, poolk_hbm, poolv_hbm, owners_ref, lengths_ref,
    out_hbm,
    page, pre_in, x, sib_s, sib_r, in_up, in_dn, up_s, up_r, dn_s, dn_r, kvf, bias, q_ref, nk_ref, nv_ref, out_ref,
    page_sems, pre_sems, load_sems, send_sems, recv_sems, out_sems,
):
    long, short = grid_of(ring)
    me = lax.axis_index("ctx")
    core = lax.rem(me, 2)
    chip = lax.div(me, 2)
    py = lax.rem(chip, short)
    pz = lax.div(chip, short)
    sibling = me + 1 - 2 * core
    sy, sz = 2, 2 * short

    barrier = pltpu.get_barrier_semaphore()

    def greet(target):
        pl.semaphore_signal(barrier, inc=1, device_id={"ctx": target})

    greet(sibling)
    peers = 1
    for pos, size, step in ((py, short, sy), (pz, long, sz)):
        @pl.when(pos > 0)
        def _():
            greet(me - step)

        @pl.when(pos < size - 1)
        def _():
            greet(me + step)

        peers = peers + jnp.where(pos > 0, 1, 0) + jnp.where(pos < size - 1, 1, 0)

    pages = poolk_hbm.shape[1]
    pieces = pages * CUTS
    page_rows = poolk_hbm.shape[2]
    blk = page_rows // CUTS
    chunks = kv_heads * pieces
    pairs = chunks // 2
    per_head = pieces // 2
    own_rows = pk_hbm.shape[0]
    pre = own_rows * ring // pieces
    rows = q_hbm.shape[0]
    group = heads // kv_heads
    width = kv_heads * HD

    splits = ((0, HD), (HD, width - HD))

    def page_copy(src, slot, part):
        start, size = splits[part]
        return pltpu.make_async_copy(
            src.at[0, :, :, pl.ds(start, size)], page.at[slot, :, :, pl.ds(start, size)], page_sems.at[slot, part]
        )

    def pre_copy(src, slot):
        return pltpu.make_async_copy(src, pre_in.at[slot], pre_sems.at[slot])

    def fetch(k_slot):
        pre_copy(pk_hbm, k_slot).start()
        pre_copy(pv_hbm, 1 - k_slot).start()
        for part in range(2):
            page_copy(poolk_hbm, k_slot, part).start()
            page_copy(poolv_hbm, 1 - k_slot, part).start()

    @pl.when(core == 0)
    def _():
        fetch(0)

    @pl.when(core == 1)
    def _():
        fetch(1)

    loads = [
        pltpu.make_async_copy(src, dst, load_sems.at[n])
        for n, (src, dst) in enumerate(((q_hbm, q_ref), (nk_hbm, nk_ref), (nv_hbm, nv_ref)))
    ]
    for load in loads:
        load.start()

    length = lengths_ref[0]
    tok = lax.broadcasted_iota(jnp.int32, (rows, rows), 0)
    key = lax.broadcasted_iota(jnp.int32, (rows, rows), 1)
    bias[...] = jnp.where((key <= tok) & (key < length), 0.0, -1e30)

    def wait_pages(part):
        for slot in range(2):
            page_copy(poolk_hbm, slot, part).wait()

    for slot in range(2):
        pre_copy(pk_hbm, slot).wait()
    wait_pages(0)
    pl.semaphore_wait(barrier, peers)

    def remote(kind, b, i, src, dst, target):
        return pltpu.make_async_remote_copy(
            src_ref=src, dst_ref=dst, send_sem=send_sems.at[kind, b], recv_sem=recv_sems.at[kind, i],
            device_id={"ctx": target}, device_id_type=pl.DeviceIdType.MESH,
        )

    def cols(g):
        return pl.ds(pl.multiple_of(g * HD, HD), HD)

    def build(i):
        g, b = lax.div(i, pieces), lax.rem(i, pieces)
        page_of = lax.div(b, CUTS)
        start = pl.multiple_of(lax.rem(b, CUTS) * blk, blk)
        mine = jnp.where(owners_ref[page_of] == me, 1.0, 0.0).astype(jnp.float32)
        row = lax.broadcasted_iota(jnp.int32, (pre, HD), 0) + b * pre
        in_mine = (row >= me * own_rows) & (row < (me + 1) * own_rows)
        for slot, dst in ((1, sib_s), (0, x)):
            part = page[slot, page_of, pl.ds(start, blk), cols(g)]
            dst[i, :blk] = part * jnp.full(part.shape, mine, jnp.float32).astype(jnp.bfloat16)
            mine_pre = pre_in[slot, :, cols(g)].astype(jnp.float32)
            tiled = jnp.concatenate([mine_pre] * (pre // own_rows), axis=0)
            dst[i, blk:] = jnp.where(in_mine, tiled, 0.0).astype(jnp.bfloat16)

    def pair(u):
        return pl.ds(2 * u, 2)

    def sib_copy(u):
        return remote(0, 0, u, sib_s.at[pair(u)], sib_r.at[pair(u)], sibling)

    def in_up_copy(b, i):
        return remote(1, b, i, x.at[i], in_up.at[i], me + sy)

    def in_dn_copy(b, i):
        return remote(2, b, i, x.at[i], in_dn.at[i], me - sy)

    def up_copy(b, i, src):
        return remote(3, b, i, src.at[i], up_r.at[i], me + sz)

    def dn_copy(b, i, src):
        return remote(4, b, i, src.at[i], dn_r.at[i], me - sz)

    def share_copy(b, i):
        return remote(5, b, i, kvf.at[core, i], kvf.at[core, i], sibling)

    def out_up_copy(b, i):
        return remote(6, b, i, kvf.at[core, i], kvf.at[core, i], me + sy)

    def out_dn_copy(b, i):
        return remote(7, b, i, kvf.at[core, i], kvf.at[core, i], me - sy)

    depth = short // 2
    roots = (depth, depth - 1 + short % 2)

    def after(hops):
        return SIB + lax.div(hops * HOP[0], HOP[1]) if not isinstance(hops, int) else SIB + hops * HOP[0] // HOP[1]

    def at(u):
        return (u >= 0) & (u < pairs)

    def gather(t):
        u = t - SIB

        @pl.when(at(u))
        def _():
            sib_copy(u).wait_recv()
            x[pair(u)] = x[pair(u)] + sib_r[pair(u)]
            for b, root in enumerate(roots):
                if root > 0:
                    @pl.when(py == 0)
                    def _():
                        in_up_copy(b, 2 * u + b).start()

                if root < short - 1:
                    @pl.when(py == short - 1)
                    def _():
                        in_dn_copy(b, 2 * u + b).start()

        for b, root in enumerate(roots):
            for hop in range(1, root):
                up = t - after(hop)

                @pl.when(at(up) & (py == hop))
                def _():
                    i = 2 * up + b
                    in_up_copy(b, i).wait_recv()
                    x[i] = x[i] + in_up[i]
                    in_up_copy(b, i).start()

            for hop in range(1, short - 1 - root):
                dn = t - after(hop)

                @pl.when(at(dn) & (py == short - 1 - hop))
                def _():
                    i = 2 * dn + b
                    in_dn_copy(b, i).wait_recv()
                    x[i] = x[i] + in_dn[i]
                    in_dn_copy(b, i).start()

    def root_hops(root):
        return max(root, short - 1 - root)

    def scan(t):
        for b, root in enumerate(roots):
            hops = root_hops(root)
            r = t - after(hops)

            @pl.when(at(r) & (py == root))
            def _():
                i = 2 * r + b
                if root > 0:
                    in_up_copy(b, i).wait_recv()
                    x[i] = x[i] + in_up[i]
                if root < short - 1:
                    in_dn_copy(b, i).wait_recv()
                    x[i] = x[i] + in_dn[i]

                if long > 1:
                    @pl.when(pz == 0)
                    def _():
                        up_copy(b, i, x).start()

                    @pl.when(pz == long - 1)
                    def _():
                        dn_copy(b, i, x).start()

            up = t - after(hops + pz)

            @pl.when(at(up) & (py == root) & (pz > 0))
            def _():
                i = 2 * up + b
                up_copy(b, i, up_s).wait_recv()

                @pl.when(pz < long - 1)
                def _():
                    up_s[i] = x[i] + up_r[i]
                    up_copy(b, i, up_s).start()

            dn = t - after(hops + long - 1 - pz)

            @pl.when(at(dn) & (py == root) & (pz < long - 1))
            def _():
                i = 2 * dn + b
                dn_copy(b, i, dn_s).wait_recv()

                @pl.when(pz > 0)
                def _():
                    dn_s[i] = x[i] + dn_r[i]
                    dn_copy(b, i, dn_s).start()

    z_hops = jnp.maximum(pz, long - 1 - pz)

    def spread(t):
        for b, root in enumerate(roots):
            hops = root_hops(root) + z_hops
            end = t - after(hops)

            @pl.when(at(end) & (py == root))
            def _():
                i = 2 * end + b

                if long == 1:
                    kvf[core, i] = x[i]
                else:
                    @pl.when((pz > 0) & (pz < long - 1))
                    def _():
                        kvf[core, i] = x[i] + up_r[i] + dn_r[i]

                    @pl.when(pz == long - 1)
                    def _():
                        kvf[core, i] = x[i] + up_r[i]

                    @pl.when(pz == 0)
                    def _():
                        kvf[core, i] = x[i] + dn_r[i]

                if root < short - 1:
                    out_up_copy(b, i).start()
                if root > 0:
                    out_dn_copy(b, i).start()
                share_copy(b, i).start()

            above = jnp.where(py > root, py - root, root - py)
            out = t - after(hops + above)

            @pl.when(at(out) & (py > root))
            def _():
                i = 2 * out + b
                out_up_copy(b, i).wait_recv()

                @pl.when(py < short - 1)
                def _():
                    out_up_copy(b, i).start()

                share_copy(b, i).start()

            @pl.when(at(out) & (py < root))
            def _():
                i = 2 * out + b
                out_dn_copy(b, i).wait_recv()

                @pl.when(py > 0)
                def _():
                    out_dn_copy(b, i).start()

                share_copy(b, i).start()

    def far(root):
        return jnp.where(py > root, py - root, root - py)

    def arrive(t):
        for b, root in enumerate(roots):
            c = t - SIB - after(root_hops(root) + z_hops + far(root))

            @pl.when(at(c))
            def _():
                i = 2 * c + b
                remote(5, b, i, kvf.at[core, i], kvf.at[1 - core, i], sibling).wait_recv()

    live = lax.broadcasted_iota(jnp.int32, (rows, HD), 0) < length
    score_scale = 1.4426950408889634 / HD**0.5
    wide = group * HD

    def result_copy(g):
        columns = pl.ds(pl.multiple_of(g * wide, wide), wide)
        return pltpu.make_async_copy(out_ref.at[:, columns], out_hbm.at[:, columns], out_sems.at[g])

    all_rows = pieces * (blk + pre)

    def attend(g):
        first = g * group
        keys = kvf[0, pl.ds(g * pieces, pieces)].reshape(all_rows, HD)
        values = kvf[1, pl.ds(g * pieces, pieces)].reshape(all_rows, HD)
        dims = (((1,), (1,)), ((), ()))
        v_far = jnp.concatenate([values, jnp.ones_like(values)], axis=1)
        own_k, own_v = nk_ref[:, cols(g)], nv_ref[:, cols(g)]
        v_own = jnp.concatenate([own_v, jnp.ones_like(own_v)], axis=1)
        mask = jnp.concatenate([bias[...]] * SUB, axis=0)
        for sub in range(0, group, SUB):
            q = jnp.concatenate([q_ref[:, cols(first + sub + j)] for j in range(SUB)], axis=0)
            s_far = lax.dot_general(q, keys, dims, preferred_element_type=jnp.float32)
            s_own = lax.dot_general(q, own_k, dims, preferred_element_type=jnp.float32) + mask
            top = jnp.maximum(jnp.max(s_far, axis=1, keepdims=True), jnp.max(s_own, axis=1, keepdims=True))
            w_far = jnp.exp2((s_far - top) * score_scale).astype(jnp.bfloat16)
            w_own = jnp.exp2((s_own - top) * score_scale).astype(jnp.bfloat16)
            summed = jnp.dot(w_far, v_far, preferred_element_type=jnp.float32)
            summed += jnp.dot(w_own, v_own, preferred_element_type=jnp.float32)
            result = summed[:, :HD] / summed[:, HD:]
            for j in range(SUB):
                piece = jnp.where(live, result[j * rows : (j + 1) * rows], 0.0)
                out_ref[:, cols(first + sub + j)] = piece.astype(out_ref.dtype)

    reach = max(root_hops(root) + max(root, short - 1 - root) for root in roots)
    done = SIB + after(reach + z_hops)
    steps = SIB + after(reach + long - 1) + pairs

    def one_step(t, carry):
        @pl.when(t == 1)
        def _():
            wait_pages(1)

        @pl.when(t < pairs)
        def _():
            build(2 * t)
            build(2 * t + 1)
            sib_copy(t).start()

        gather(t)
        scan(t)
        spread(t)
        arrive(t)

        @pl.when(t == SIB + 1)
        def _():
            for load in loads:
                load.wait()

        u = t - done

        @pl.when(at(u) & (lax.rem(u, per_head) == per_head - 1))
        def _():
            g = lax.div(u, per_head)
            attend(g)
            result_copy(g).start()

        return carry

    lax.fori_loop(0, steps, one_step, 0)

    half = pl.ds(0, pairs)
    every = pl.ds(0, chunks)
    remote(0, 0, 0, sib_s.at[every], sib_r.at[every], sibling).wait_send()
    for b, root in enumerate(roots):
        for kind, used in (
            (1, py < root),
            (2, py > root),
            (3, (py == root) & (pz < long - 1)),
            (4, (py == root) & (pz > 0)),
            (5, py >= 0),
            (6, (py >= root) & (py < short - 1)),
            (7, (py <= root) & (py > 0)),
        ):
            @pl.when(used)
            def _():
                remote(kind, b, 0, x.at[half], sib_r.at[half], sibling).wait_send()

    for g in range(kv_heads):
        result_copy(g).wait()


def solution(mesh):
    ring = mesh.shape["ctx"]

    def body(queries, new_keys, new_values, prefix_keys, prefix_values, pool_keys, pool_values, owners, lengths):
        heads = queries.shape[1] // HD
        kv_heads = new_keys.shape[1] // HD
        pages, page_rows = pool_keys.shape[1:3]
        pieces = pages * CUTS
        chunks = kv_heads * pieces
        c_rows = page_rows // CUTS + prefix_keys.shape[0] * ring // pieces
        chunk_buf = pltpu.VMEM((chunks, c_rows, HD), jnp.bfloat16)
        hbm = pl.BlockSpec(memory_space=pl.ANY)
        sm = pl.BlockSpec(memory_space=pltpu.SMEM)
        return pl.pallas_call(
            functools.partial(kernel, ring, heads, kv_heads),
            out_shape=jax.ShapeDtypeStruct(queries.shape, jnp.bfloat16),
            in_specs=[hbm] * 7 + [sm] * 2,
            out_specs=hbm,
            scratch_shapes=[
                pltpu.VMEM((2, pages, page_rows, kv_heads * HD), jnp.bfloat16),
                pltpu.VMEM((2,) + prefix_keys.shape, jnp.bfloat16),
            ]
            + [chunk_buf] * 9
            + [
                pltpu.VMEM((2, chunks, c_rows, HD), jnp.bfloat16),
                pltpu.VMEM((queries.shape[0], queries.shape[0]), jnp.float32),
                pltpu.VMEM(queries.shape, jnp.bfloat16),
                pltpu.VMEM(new_keys.shape, jnp.bfloat16),
                pltpu.VMEM(new_values.shape, jnp.bfloat16),
                pltpu.VMEM(queries.shape, jnp.bfloat16),
                pltpu.SemaphoreType.DMA((2, 2)),
                pltpu.SemaphoreType.DMA((2,)),
                pltpu.SemaphoreType.DMA((3,)),
                pltpu.SemaphoreType.DMA((8, 2)),
                pltpu.SemaphoreType.DMA((8, chunks)),
                pltpu.SemaphoreType.DMA((kv_heads,)),
            ],
            compiler_params=pltpu.CompilerParams(
                collective_id=0, has_side_effects=True, vmem_limit_bytes=67043328
            ),
        )(queries, new_keys, new_values, prefix_keys, prefix_values, pool_keys, pool_values, owners, lengths)

    two = P(("groups", "ctx"), None)
    four = P(("groups", "ctx"), None, None, None)
    return jax.shard_map(
        body, mesh=mesh, in_specs=(two,) * 5 + (four,) * 2 + (P("groups"), P(("groups", "ctx"))),
        out_specs=two, check_vma=False,
    )
```

```python
import functools

import jax
import jax.numpy as jnp
from jax import lax
from jax.experimental import pallas as pl
from jax.experimental.pallas import tpu as pltpu
from jax.sharding import PartitionSpec as P

HD = 128
CUTS = 1
SIB = 1
HOP = (3, 1)
SUB = 4
PRE_STEPS = (2, 5, 6)
NEAR_STEP = 7


def grid_of(ring):
    chips = ring // 2
    short = 1
    while (short * 2) ** 2 <= chips and chips % (short * 2) == 0:
        short *= 2
    return chips // short, short


def kernel(
    ring, heads, kv_heads,
    q_hbm, nk_hbm, nv_hbm, pk_hbm, pv_hbm, poolk_hbm, poolv_hbm, owners_ref, lengths_ref,
    out_hbm,
    page, pref, x, sib_s, sib_r, in_up, in_dn, up_s, up_r, dn_s, dn_r, kvf, bias, q_ref, nk_ref, nv_ref, out_ref, near_sum, near_top,
    page_sems, load_sems, pre_send, pre_recv, send_sems, recv_sems, out_sems,
):
    long, short = grid_of(ring)
    me = lax.axis_index("ctx")
    core = lax.rem(me, 2)
    chip = lax.div(me, 2)
    py = lax.rem(chip, short)
    pz = lax.div(chip, short)
    sibling = me + 1 - 2 * core
    sy, sz = 2, 2 * short

    barrier = pltpu.get_barrier_semaphore()

    def greet(target):
        pl.semaphore_signal(barrier, inc=1, device_id={"ctx": target})

    def y_peer(d):
        return me + (lax.rem(py + d, short) - py) * sy

    def z_peer(d):
        return me + (lax.rem(pz + d, long) - pz) * sz

    greet(sibling)
    for d in range(1, short):
        greet(y_peer(d))
    for d in range(1, long):
        greet(z_peer(d))
    peers = 1 + short - 1 + long - 1

    pages = poolk_hbm.shape[1]
    pieces = pages * CUTS
    page_rows = poolk_hbm.shape[2]
    blk = page_rows // CUTS
    chunks = kv_heads * pieces
    pairs = chunks // 2
    per_head = pieces // 2
    own_rows = pk_hbm.shape[0]
    pre = own_rows * ring
    rows = q_hbm.shape[0]
    group = heads // kv_heads
    width = kv_heads * HD

    splits = ((0, HD), (HD, width - HD))

    def page_copy(src, slot, part):
        start, size = splits[part]
        return pltpu.make_async_copy(
            src.at[0, :, :, pl.ds(start, size)], page.at[slot, :, :, pl.ds(start, size)], page_sems.at[slot, part]
        )

    def fetch(k_slot):
        for part in range(2):
            page_copy(poolk_hbm, k_slot, part).start()
            page_copy(poolv_hbm, 1 - k_slot, part).start()

    @pl.when(core == 0)
    def _():
        fetch(0)

    @pl.when(core == 1)
    def _():
        fetch(1)

    mine = pref.at[core, pz, py]
    own_pre = [pltpu.make_async_copy(src, mine.at[n], load_sems.at[n]) for n, src in enumerate((pk_hbm, pv_hbm))]
    for load in own_pre:
        load.start()

    loads = [
        pltpu.make_async_copy(src, dst, load_sems.at[n])
        for n, (src, dst) in enumerate(((q_hbm, q_ref), (nk_hbm, nk_ref), (nv_hbm, nv_ref)), start=2)
    ]
    for load in loads:
        load.start()

    length = lengths_ref[0]
    tok = lax.broadcasted_iota(jnp.int32, (rows, rows), 0)
    key = lax.broadcasted_iota(jnp.int32, (rows, rows), 1)
    bias[...] = jnp.where((key <= tok) & (key < length), 0.0, -1e30)

    def wait_pages(part):
        for slot in range(2):
            page_copy(poolk_hbm, slot, part).wait()

    def pre_y(d, source):
        return pltpu.make_async_remote_copy(
            src_ref=mine, dst_ref=mine, send_sem=pre_send.at[source], recv_sem=pre_recv.at[source],
            device_id={"ctx": y_peer(d)}, device_id_type=pl.DeviceIdType.MESH,
        )

    def pre_z(d, source):
        row = pref.at[core, pz]
        return pltpu.make_async_remote_copy(
            src_ref=row, dst_ref=row, send_sem=pre_send.at[short + source], recv_sem=pre_recv.at[short + source],
            device_id={"ctx": z_peer(d)}, device_id_type=pl.DeviceIdType.MESH,
        )

    def pre_sib(slot):
        return pltpu.make_async_remote_copy(
            src_ref=pref.at[slot], dst_ref=pref.at[slot], send_sem=pre_send.at[short + long], recv_sem=pre_recv.at[short + long],
            device_id={"ctx": sibling}, device_id_type=pl.DeviceIdType.MESH,
        )

    def pre_step(n):
        if n == 0:
            for d in range(1, short):
                pltpu.make_async_remote_copy(
                    src_ref=mine, dst_ref=pref.at[core, pz, lax.rem(py + short - d, short)], send_sem=pre_send.at[d],
                    recv_sem=pre_recv.at[d], device_id={"ctx": y_peer(d)}, device_id_type=pl.DeviceIdType.MESH,
                ).wait_recv()
            for d in range(1, long):
                pre_z(d, d).start()
        elif n == 1:
            for d in range(1, long):
                pltpu.make_async_remote_copy(
                    src_ref=pref.at[core, pz], dst_ref=pref.at[core, lax.rem(pz + long - d, long)], send_sem=pre_send.at[short + d],
                    recv_sem=pre_recv.at[short + d], device_id={"ctx": z_peer(d)}, device_id_type=pl.DeviceIdType.MESH,
                ).wait_recv()
            pre_sib(core).start()
        else:
            pre_sib(1 - core).wait_recv()

    for load in own_pre:
        load.wait()
    wait_pages(0)
    pl.semaphore_wait(barrier, peers)
    for d in range(1, short):
        pre_y(d, d).start()

    def remote(kind, b, i, src, dst, target):
        return pltpu.make_async_remote_copy(
            src_ref=src, dst_ref=dst, send_sem=send_sems.at[kind, b], recv_sem=recv_sems.at[kind, i],
            device_id={"ctx": target}, device_id_type=pl.DeviceIdType.MESH,
        )

    def cols(g):
        return pl.ds(pl.multiple_of(g * HD, HD), HD)

    def build(i):
        g, b = lax.div(i, pieces), lax.rem(i, pieces)
        page_of = lax.div(b, CUTS)
        start = pl.multiple_of(lax.rem(b, CUTS) * blk, blk)
        held = jnp.where(owners_ref[page_of] == me, 1.0, 0.0).astype(jnp.float32)
        for slot, dst in ((1, sib_s), (0, x)):
            part = page[slot, page_of, pl.ds(start, blk), cols(g)]
            dst[i] = part * jnp.full(part.shape, held, jnp.float32).astype(jnp.bfloat16)

    def pair(u):
        return pl.ds(2 * u, 2)

    def sib_copy(u):
        return remote(0, 0, u, sib_s.at[pair(u)], sib_r.at[pair(u)], sibling)

    def in_up_copy(b, i):
        return remote(1, b, i, x.at[i], in_up.at[i], me + sy)

    def in_dn_copy(b, i):
        return remote(2, b, i, x.at[i], in_dn.at[i], me - sy)

    def up_copy(b, i, src):
        return remote(3, b, i, src.at[i], up_r.at[i], me + sz)

    def dn_copy(b, i, src):
        return remote(4, b, i, src.at[i], dn_r.at[i], me - sz)

    def share_copy(b, i):
        return remote(5, b, i, kvf.at[core, i], kvf.at[core, i], sibling)

    def out_up_copy(b, i):
        return remote(6, b, i, kvf.at[core, i], kvf.at[core, i], me + sy)

    def out_dn_copy(b, i):
        return remote(7, b, i, kvf.at[core, i], kvf.at[core, i], me - sy)

    depth = short // 2
    roots = (depth, depth - 1 + short % 2)

    def after(hops):
        return SIB + lax.div(hops * HOP[0], HOP[1]) if not isinstance(hops, int) else SIB + hops * HOP[0] // HOP[1]

    def at(u):
        return (u >= 0) & (u < pairs)

    def gather(t):
        u = t - SIB

        @pl.when(at(u))
        def _():
            sib_copy(u).wait_recv()
            x[pair(u)] = x[pair(u)] + sib_r[pair(u)]
            for b, root in enumerate(roots):
                if root > 0:
                    @pl.when(py == 0)
                    def _():
                        in_up_copy(b, 2 * u + b).start()

                if root < short - 1:
                    @pl.when(py == short - 1)
                    def _():
                        in_dn_copy(b, 2 * u + b).start()

        for b, root in enumerate(roots):
            for hop in range(1, root):
                up = t - after(hop)

                @pl.when(at(up) & (py == hop))
                def _():
                    i = 2 * up + b
                    in_up_copy(b, i).wait_recv()
                    x[i] = x[i] + in_up[i]
                    in_up_copy(b, i).start()

            for hop in range(1, short - 1 - root):
                dn = t - after(hop)

                @pl.when(at(dn) & (py == short - 1 - hop))
                def _():
                    i = 2 * dn + b
                    in_dn_copy(b, i).wait_recv()
                    x[i] = x[i] + in_dn[i]
                    in_dn_copy(b, i).start()

    def root_hops(root):
        return max(root, short - 1 - root)

    def scan(t):
        for b, root in enumerate(roots):
            hops = root_hops(root)
            r = t - after(hops)

            @pl.when(at(r) & (py == root))
            def _():
                i = 2 * r + b
                if root > 0:
                    in_up_copy(b, i).wait_recv()
                    x[i] = x[i] + in_up[i]
                if root < short - 1:
                    in_dn_copy(b, i).wait_recv()
                    x[i] = x[i] + in_dn[i]

                if long > 1:
                    @pl.when(pz == 0)
                    def _():
                        up_copy(b, i, x).start()

                    @pl.when(pz == long - 1)
                    def _():
                        dn_copy(b, i, x).start()

            up = t - after(hops + pz)

            @pl.when(at(up) & (py == root) & (pz > 0))
            def _():
                i = 2 * up + b
                up_copy(b, i, up_s).wait_recv()

                @pl.when(pz < long - 1)
                def _():
                    up_s[i] = x[i] + up_r[i]
                    up_copy(b, i, up_s).start()

            dn = t - after(hops + long - 1 - pz)

            @pl.when(at(dn) & (py == root) & (pz < long - 1))
            def _():
                i = 2 * dn + b
                dn_copy(b, i, dn_s).wait_recv()

                @pl.when(pz > 0)
                def _():
                    dn_s[i] = x[i] + dn_r[i]
                    dn_copy(b, i, dn_s).start()

    z_hops = jnp.maximum(pz, long - 1 - pz)

    def spread(t):
        for b, root in enumerate(roots):
            hops = root_hops(root) + z_hops
            end = t - after(hops)

            @pl.when(at(end) & (py == root))
            def _():
                i = 2 * end + b

                if long == 1:
                    kvf[core, i] = x[i]
                else:
                    @pl.when((pz > 0) & (pz < long - 1))
                    def _():
                        kvf[core, i] = x[i] + up_r[i] + dn_r[i]

                    @pl.when(pz == long - 1)
                    def _():
                        kvf[core, i] = x[i] + up_r[i]

                    @pl.when(pz == 0)
                    def _():
                        kvf[core, i] = x[i] + dn_r[i]

                if root < short - 1:
                    out_up_copy(b, i).start()
                if root > 0:
                    out_dn_copy(b, i).start()
                share_copy(b, i).start()

            above = jnp.where(py > root, py - root, root - py)
            out = t - after(hops + above)

            @pl.when(at(out) & (py > root))
            def _():
                i = 2 * out + b
                out_up_copy(b, i).wait_recv()

                @pl.when(py < short - 1)
                def _():
                    out_up_copy(b, i).start()

                share_copy(b, i).start()

            @pl.when(at(out) & (py < root))
            def _():
                i = 2 * out + b
                out_dn_copy(b, i).wait_recv()

                @pl.when(py > 0)
                def _():
                    out_dn_copy(b, i).start()

                share_copy(b, i).start()

    def far(root):
        return jnp.where(py > root, py - root, root - py)

    def arrive(t):
        for b, root in enumerate(roots):
            c = t - SIB - after(root_hops(root) + z_hops + far(root))

            @pl.when(at(c))
            def _():
                i = 2 * c + b
                remote(5, b, i, kvf.at[core, i], kvf.at[1 - core, i], sibling).wait_recv()

    live = lax.broadcasted_iota(jnp.int32, (rows, HD), 0) < length
    score_scale = 1.4426950408889634 / HD**0.5
    wide = group * HD

    def result_copy(g):
        columns = pl.ds(pl.multiple_of(g * wide, wide), wide)
        return pltpu.make_async_copy(out_ref.at[:, columns], out_hbm.at[:, columns], out_sems.at[g])

    all_rows = pieces * blk

    dims = (((1,), (1,)), ((), ()))

    def with_ones(values):
        return jnp.concatenate([values, jnp.ones_like(values)], axis=1)

    def query_rows(head):
        return jnp.concatenate([q_ref[:, cols(head + j)] for j in range(SUB)], axis=0)

    def near(g):
        keys = jnp.concatenate([pref[:, :, :, 0, :, cols(g)].reshape(pre, HD), nk_ref[:, cols(g)]], axis=0)
        values = jnp.concatenate([pref[:, :, :, 1, :, cols(g)].reshape(pre, HD), nv_ref[:, cols(g)]], axis=0)
        values = with_ones(values)
        mask = jnp.concatenate([jnp.zeros((rows, pre), jnp.float32), bias[...]], axis=1)
        mask = jnp.concatenate([mask] * SUB, axis=0)
        for sub in range(0, group, SUB):
            scores = lax.dot_general(query_rows(g * group + sub), keys, dims, preferred_element_type=jnp.float32) + mask
            top = jnp.max(scores, axis=1, keepdims=True)
            weights = jnp.exp2((scores - top) * score_scale).astype(jnp.bfloat16)
            part = pl.ds(sub * rows, SUB * rows)
            near_sum[g, part] = jnp.dot(weights, values, preferred_element_type=jnp.float32)
            near_top[g, part] = jnp.broadcast_to(top, (SUB * rows, HD))

    def attend(g):
        keys = kvf[0, pl.ds(g * pieces, pieces)].reshape(all_rows, HD)
        values = with_ones(kvf[1, pl.ds(g * pieces, pieces)].reshape(all_rows, HD))
        for sub in range(0, group, SUB):
            scores = lax.dot_general(query_rows(g * group + sub), keys, dims, preferred_element_type=jnp.float32)
            part = pl.ds(sub * rows, SUB * rows)
            before = near_top[g, part]
            top = jnp.maximum(jnp.max(scores, axis=1, keepdims=True), before)
            wide_top = jnp.concatenate([top] * (all_rows // HD), axis=1)
            weights = jnp.exp2((scores - wide_top) * score_scale).astype(jnp.bfloat16)
            scale = jnp.exp2((before - top) * score_scale)
            summed = jnp.dot(weights, values, preferred_element_type=jnp.float32)
            summed += jnp.concatenate([scale, scale], axis=1) * near_sum[g, part]
            result = summed[:, :HD] / summed[:, HD:]
            for j in range(SUB):
                piece = jnp.where(live, result[j * rows : (j + 1) * rows], 0.0)
                out_ref[:, cols(g * group + sub + j)] = piece.astype(out_ref.dtype)

    reach = max(root_hops(root) + max(root, short - 1 - root) for root in roots)
    done = SIB + after(reach + z_hops)
    steps = SIB + after(reach + long - 1) + pairs

    def one_step(t, carry):
        @pl.when(t == 1)
        def _():
            wait_pages(1)

        @pl.when(t < pairs)
        def _():
            build(2 * t)
            build(2 * t + 1)
            sib_copy(t).start()

        @pl.when(t == SIB + 1)
        def _():
            for load in loads:
                load.wait()

        ahead = t - NEAR_STEP

        @pl.when((ahead >= 0) & (ahead < kv_heads))
        def _():
            near(ahead)

        gather(t)
        scan(t)
        spread(t)
        arrive(t)

        for n in range(3):
            @pl.when(t == PRE_STEPS[n])
            def _():
                pre_step(n)

        u = t - done

        @pl.when(at(u) & (lax.rem(u, per_head) == per_head - 1))
        def _():
            g = lax.div(u, per_head)
            attend(g)
            result_copy(g).start()

        return carry

    lax.fori_loop(0, steps, one_step, 0)

    for d in range(1, short):
        pre_y(d, d).wait_send()
    for d in range(1, long):
        pre_z(d, d).wait_send()
    pre_sib(core).wait_send()
    half = pl.ds(0, pairs)
    every = pl.ds(0, chunks)
    remote(0, 0, 0, sib_s.at[every], sib_r.at[every], sibling).wait_send()
    for b, root in enumerate(roots):
        for kind, used in (
            (1, py < root),
            (2, py > root),
            (3, (py == root) & (pz < long - 1)),
            (4, (py == root) & (pz > 0)),
            (5, py >= 0),
            (6, (py >= root) & (py < short - 1)),
            (7, (py <= root) & (py > 0)),
        ):
            @pl.when(used)
            def _():
                remote(kind, b, 0, x.at[half], sib_r.at[half], sibling).wait_send()

    for g in range(kv_heads):
        result_copy(g).wait()


def solution(mesh):
    ring = mesh.shape["ctx"]

    def body(queries, new_keys, new_values, prefix_keys, prefix_values, pool_keys, pool_values, owners, lengths):
        heads = queries.shape[1] // HD
        kv_heads = new_keys.shape[1] // HD
        pages, page_rows = pool_keys.shape[1:3]
        pieces = pages * CUTS
        chunks = kv_heads * pieces
        c_rows = page_rows // CUTS
        long, short = grid_of(ring)
        chunk_buf = pltpu.VMEM((chunks, c_rows, HD), jnp.bfloat16)
        hbm = pl.BlockSpec(memory_space=pl.ANY)
        sm = pl.BlockSpec(memory_space=pltpu.SMEM)
        return pl.pallas_call(
            functools.partial(kernel, ring, heads, kv_heads),
            out_shape=jax.ShapeDtypeStruct(queries.shape, jnp.bfloat16),
            in_specs=[hbm] * 7 + [sm] * 2,
            out_specs=hbm,
            scratch_shapes=[
                pltpu.VMEM((2, pages, page_rows, kv_heads * HD), jnp.bfloat16),
                pltpu.VMEM((2, long, short, 2) + prefix_keys.shape, jnp.bfloat16),
            ]
            + [chunk_buf] * 9
            + [
                pltpu.VMEM((2, chunks, c_rows, HD), jnp.bfloat16),
                pltpu.VMEM((queries.shape[0], queries.shape[0]), jnp.float32),
                pltpu.VMEM(queries.shape, jnp.bfloat16),
                pltpu.VMEM(new_keys.shape, jnp.bfloat16),
                pltpu.VMEM(new_values.shape, jnp.bfloat16),
                pltpu.VMEM(queries.shape, jnp.bfloat16),
                pltpu.VMEM((kv_heads, queries.shape[0] * heads // kv_heads, 2 * HD), jnp.float32),
                pltpu.VMEM((kv_heads, queries.shape[0] * heads // kv_heads, HD), jnp.float32),
                pltpu.SemaphoreType.DMA((2, 2)),
                pltpu.SemaphoreType.DMA((5,)),
                pltpu.SemaphoreType.DMA((short + long + 1,)),
                pltpu.SemaphoreType.DMA((short + long + 1,)),
                pltpu.SemaphoreType.DMA((8, 2)),
                pltpu.SemaphoreType.DMA((8, chunks)),
                pltpu.SemaphoreType.DMA((kv_heads,)),
            ],
            compiler_params=pltpu.CompilerParams(
                collective_id=0, has_side_effects=True, vmem_limit_bytes=67043328
            ),
        )(queries, new_keys, new_values, prefix_keys, prefix_values, pool_keys, pool_values, owners, lengths)

    two = P(("groups", "ctx"), None)
    four = P(("groups", "ctx"), None, None, None)
    return jax.shard_map(
        body, mesh=mesh, in_specs=(two,) * 5 + (four,) * 2 + (P("groups"), P(("groups", "ctx"))),
        out_specs=two, check_vma=False,
    )
```

```python
import functools

import jax
import jax.numpy as jnp
from jax import lax
from jax.experimental import pallas as pl
from jax.experimental.pallas import tpu as pltpu
from jax.sharding import PartitionSpec as P

HD = 128
CUTS = 1
SIB = 1
HOP = (3, 1)
SUB = 4
PRE_STEPS = (2, 5, 6)
NEAR_STEP = 7
STORES = 4


def grid_of(ring):
    chips = ring // 2
    short = 1
    while (short * 2) ** 2 <= chips and chips % (short * 2) == 0:
        short *= 2
    return chips // short, short


def kernel(
    ring, heads, kv_heads,
    q_hbm, nk_hbm, nv_hbm, pk_hbm, pv_hbm, poolk_hbm, poolv_hbm, owners_ref, lengths_ref,
    out_ref,
    page, pref, x, sib_s, sib_r, in_up, in_dn, up_s, up_r, dn_s, dn_r, kvf, bias, q_ref, nk_ref, nv_ref, near_sum, near_top,
    page_sems, load_sems, pre_send, pre_recv, send_sems, recv_sems,
):
    long, short = grid_of(ring)
    me = lax.axis_index("ctx")
    core = lax.rem(me, 2)
    chip = lax.div(me, 2)
    py = lax.rem(chip, short)
    pz = lax.div(chip, short)
    sibling = me + 1 - 2 * core
    sy, sz = 2, 2 * short

    barrier = pltpu.get_barrier_semaphore()

    def greet(target):
        pl.semaphore_signal(barrier, inc=1, device_id={"ctx": target})

    def y_peer(d):
        return me + (lax.rem(py + d, short) - py) * sy

    def z_peer(d):
        return me + (lax.rem(pz + d, long) - pz) * sz

    greet(sibling)
    for d in range(1, short):
        greet(y_peer(d))
    for d in range(1, long):
        greet(z_peer(d))
    peers = 1 + short - 1 + long - 1

    pages = poolk_hbm.shape[1]
    pieces = pages * CUTS
    page_rows = poolk_hbm.shape[2]
    blk = page_rows // CUTS
    chunks = kv_heads * pieces
    pairs = chunks // 2
    per_head = pieces // 2
    own_rows = pk_hbm.shape[0]
    pre = own_rows * ring
    rows = q_hbm.shape[0]
    group = heads // kv_heads
    width = kv_heads * HD

    splits = ((0, HD), (HD, width - HD))

    def page_copy(src, slot, part):
        start, size = splits[part]
        return pltpu.make_async_copy(
            src.at[0, :, :, pl.ds(start, size)], page.at[slot, :, :, pl.ds(start, size)], page_sems.at[slot, part]
        )

    def fetch(k_slot):
        for part in range(2):
            page_copy(poolk_hbm, k_slot, part).start()
            page_copy(poolv_hbm, 1 - k_slot, part).start()

    @pl.when(core == 0)
    def _():
        fetch(0)

    @pl.when(core == 1)
    def _():
        fetch(1)

    mine = pref.at[core, pz, py]
    own_pre = [pltpu.make_async_copy(src, mine.at[n], load_sems.at[n]) for n, src in enumerate((pk_hbm, pv_hbm))]
    for load in own_pre:
        load.start()

    loads = [
        pltpu.make_async_copy(src, dst, load_sems.at[n])
        for n, (src, dst) in enumerate(((q_hbm, q_ref), (nk_hbm, nk_ref), (nv_hbm, nv_ref)), start=2)
    ]
    for load in loads:
        load.start()

    length = lengths_ref[0]
    tok = lax.broadcasted_iota(jnp.int32, (rows, rows), 0)
    key = lax.broadcasted_iota(jnp.int32, (rows, rows), 1)
    bias[...] = jnp.where((key <= tok) & (key < length), 0.0, -1e30)

    def wait_pages(part):
        for slot in range(2):
            page_copy(poolk_hbm, slot, part).wait()

    def pre_y(d, source):
        return pltpu.make_async_remote_copy(
            src_ref=mine, dst_ref=mine, send_sem=pre_send.at[source], recv_sem=pre_recv.at[source],
            device_id={"ctx": y_peer(d)}, device_id_type=pl.DeviceIdType.MESH,
        )

    def pre_z(d, source):
        row = pref.at[core, pz]
        return pltpu.make_async_remote_copy(
            src_ref=row, dst_ref=row, send_sem=pre_send.at[short + source], recv_sem=pre_recv.at[short + source],
            device_id={"ctx": z_peer(d)}, device_id_type=pl.DeviceIdType.MESH,
        )

    def pre_sib(slot):
        return pltpu.make_async_remote_copy(
            src_ref=pref.at[slot], dst_ref=pref.at[slot], send_sem=pre_send.at[short + long], recv_sem=pre_recv.at[short + long],
            device_id={"ctx": sibling}, device_id_type=pl.DeviceIdType.MESH,
        )

    def pre_step(n):
        if n == 0:
            for d in range(1, short):
                pltpu.make_async_remote_copy(
                    src_ref=mine, dst_ref=pref.at[core, pz, lax.rem(py + short - d, short)], send_sem=pre_send.at[d],
                    recv_sem=pre_recv.at[d], device_id={"ctx": y_peer(d)}, device_id_type=pl.DeviceIdType.MESH,
                ).wait_recv()
            for d in range(1, long):
                pre_z(d, d).start()
        elif n == 1:
            for d in range(1, long):
                pltpu.make_async_remote_copy(
                    src_ref=pref.at[core, pz], dst_ref=pref.at[core, lax.rem(pz + long - d, long)], send_sem=pre_send.at[short + d],
                    recv_sem=pre_recv.at[short + d], device_id={"ctx": z_peer(d)}, device_id_type=pl.DeviceIdType.MESH,
                ).wait_recv()
            pre_sib(core).start()
        else:
            pre_sib(1 - core).wait_recv()

    for load in own_pre:
        load.wait()
    wait_pages(0)
    pl.semaphore_wait(barrier, peers)
    for d in range(1, short):
        pre_y(d, d).start()

    def remote(kind, b, i, src, dst, target):
        return pltpu.make_async_remote_copy(
            src_ref=src, dst_ref=dst, send_sem=send_sems.at[kind, b], recv_sem=recv_sems.at[kind, i],
            device_id={"ctx": target}, device_id_type=pl.DeviceIdType.MESH,
        )

    def cols(g):
        return pl.ds(pl.multiple_of(g * HD, HD), HD)

    def build(i):
        g, b = lax.div(i, pieces), lax.rem(i, pieces)
        page_of = lax.div(b, CUTS)
        start = pl.multiple_of(lax.rem(b, CUTS) * blk, blk)
        held = jnp.where(owners_ref[page_of] == me, 1.0, 0.0).astype(jnp.float32)
        for slot, dst in ((1, sib_s), (0, x)):
            part = page[slot, page_of, pl.ds(start, blk), cols(g)]
            dst[i] = part * jnp.full(part.shape, held, jnp.float32).astype(jnp.bfloat16)

    def pair(u):
        return pl.ds(2 * u, 2)

    def sib_copy(u):
        return remote(0, 0, u, sib_s.at[pair(u)], sib_r.at[pair(u)], sibling)

    def in_up_copy(b, i):
        return remote(1, b, i, x.at[i], in_up.at[i], me + sy)

    def in_dn_copy(b, i):
        return remote(2, b, i, x.at[i], in_dn.at[i], me - sy)

    def up_copy(b, i, src):
        return remote(3, b, i, src.at[i], up_r.at[i], me + sz)

    def dn_copy(b, i, src):
        return remote(4, b, i, src.at[i], dn_r.at[i], me - sz)

    def share_copy(b, i):
        return remote(5, b, i, kvf.at[core, i], kvf.at[core, i], sibling)

    def out_up_copy(b, i):
        return remote(6, b, i, kvf.at[core, i], kvf.at[core, i], me + sy)

    def out_dn_copy(b, i):
        return remote(7, b, i, kvf.at[core, i], kvf.at[core, i], me - sy)

    depth = short // 2
    roots = (depth, depth - 1 + short % 2)

    def after(hops):
        return SIB + lax.div(hops * HOP[0], HOP[1]) if not isinstance(hops, int) else SIB + hops * HOP[0] // HOP[1]

    def at(u):
        return (u >= 0) & (u < pairs)

    def gather(t):
        u = t - SIB

        @pl.when(at(u))
        def _():
            sib_copy(u).wait_recv()
            x[pair(u)] = x[pair(u)] + sib_r[pair(u)]
            for b, root in enumerate(roots):
                if root > 0:
                    @pl.when(py == 0)
                    def _():
                        in_up_copy(b, 2 * u + b).start()

                if root < short - 1:
                    @pl.when(py == short - 1)
                    def _():
                        in_dn_copy(b, 2 * u + b).start()

        for b, root in enumerate(roots):
            for hop in range(1, root):
                up = t - after(hop)

                @pl.when(at(up) & (py == hop))
                def _():
                    i = 2 * up + b
                    in_up_copy(b, i).wait_recv()
                    x[i] = x[i] + in_up[i]
                    in_up_copy(b, i).start()

            for hop in range(1, short - 1 - root):
                dn = t - after(hop)

                @pl.when(at(dn) & (py == short - 1 - hop))
                def _():
                    i = 2 * dn + b
                    in_dn_copy(b, i).wait_recv()
                    x[i] = x[i] + in_dn[i]
                    in_dn_copy(b, i).start()

    def root_hops(root):
        return max(root, short - 1 - root)

    def scan(t):
        for b, root in enumerate(roots):
            hops = root_hops(root)
            r = t - after(hops)

            @pl.when(at(r) & (py == root))
            def _():
                i = 2 * r + b
                if root > 0:
                    in_up_copy(b, i).wait_recv()
                    x[i] = x[i] + in_up[i]
                if root < short - 1:
                    in_dn_copy(b, i).wait_recv()
                    x[i] = x[i] + in_dn[i]

                if long > 1:
                    @pl.when(pz == 0)
                    def _():
                        up_copy(b, i, x).start()

                    @pl.when(pz == long - 1)
                    def _():
                        dn_copy(b, i, x).start()

            up = t - after(hops + pz)

            @pl.when(at(up) & (py == root) & (pz > 0))
            def _():
                i = 2 * up + b
                up_copy(b, i, up_s).wait_recv()

                @pl.when(pz < long - 1)
                def _():
                    up_s[i] = x[i] + up_r[i]
                    up_copy(b, i, up_s).start()

            dn = t - after(hops + long - 1 - pz)

            @pl.when(at(dn) & (py == root) & (pz < long - 1))
            def _():
                i = 2 * dn + b
                dn_copy(b, i, dn_s).wait_recv()

                @pl.when(pz > 0)
                def _():
                    dn_s[i] = x[i] + dn_r[i]
                    dn_copy(b, i, dn_s).start()

    z_hops = jnp.maximum(pz, long - 1 - pz)

    def spread(t):
        for b, root in enumerate(roots):
            hops = root_hops(root) + z_hops
            end = t - after(hops)

            @pl.when(at(end) & (py == root))
            def _():
                i = 2 * end + b

                if long == 1:
                    kvf[core, i] = x[i]
                else:
                    @pl.when((pz > 0) & (pz < long - 1))
                    def _():
                        kvf[core, i] = x[i] + up_r[i] + dn_r[i]

                    @pl.when(pz == long - 1)
                    def _():
                        kvf[core, i] = x[i] + up_r[i]

                    @pl.when(pz == 0)
                    def _():
                        kvf[core, i] = x[i] + dn_r[i]

                if root < short - 1:
                    out_up_copy(b, i).start()
                if root > 0:
                    out_dn_copy(b, i).start()
                share_copy(b, i).start()

            above = jnp.where(py > root, py - root, root - py)
            out = t - after(hops + above)

            @pl.when(at(out) & (py > root))
            def _():
                i = 2 * out + b
                out_up_copy(b, i).wait_recv()

                @pl.when(py < short - 1)
                def _():
                    out_up_copy(b, i).start()

                share_copy(b, i).start()

            @pl.when(at(out) & (py < root))
            def _():
                i = 2 * out + b
                out_dn_copy(b, i).wait_recv()

                @pl.when(py > 0)
                def _():
                    out_dn_copy(b, i).start()

                share_copy(b, i).start()

    def far(root):
        return jnp.where(py > root, py - root, root - py)

    def arrive(t):
        for b, root in enumerate(roots):
            c = t - SIB - after(root_hops(root) + z_hops + far(root))

            @pl.when(at(c))
            def _():
                i = 2 * c + b
                remote(5, b, i, kvf.at[core, i], kvf.at[1 - core, i], sibling).wait_recv()

    live = lax.broadcasted_iota(jnp.int32, (rows, HD), 0) < length
    score_scale = 1.4426950408889634 / HD**0.5
    all_rows = pieces * blk

    dims = (((1,), (1,)), ((), ()))

    def with_ones(values):
        return jnp.concatenate([values, jnp.ones_like(values)], axis=1)

    def query_rows(head):
        return jnp.concatenate([q_ref[:, cols(head + j)] for j in range(SUB)], axis=0)

    def near(g):
        keys = jnp.concatenate([pref[:, :, :, 0, :, cols(g)].reshape(pre, HD), nk_ref[:, cols(g)]], axis=0)
        values = jnp.concatenate([pref[:, :, :, 1, :, cols(g)].reshape(pre, HD), nv_ref[:, cols(g)]], axis=0)
        values = with_ones(values)
        mask = jnp.concatenate([jnp.zeros((rows, pre), jnp.float32), bias[...]], axis=1)
        mask = jnp.concatenate([mask] * SUB, axis=0)
        for sub in range(0, group, SUB):
            scores = lax.dot_general(query_rows(g * group + sub), keys, dims, preferred_element_type=jnp.float32) + mask
            top = jnp.max(scores, axis=1, keepdims=True)
            weights = jnp.exp2((scores - top) * score_scale).astype(jnp.bfloat16)
            part = pl.ds(sub * rows, SUB * rows)
            near_sum[g, part] = jnp.dot(weights, values, preferred_element_type=jnp.float32)
            near_top[g, part] = jnp.broadcast_to(top, (SUB * rows, HD))

    def attend(g):
        keys = kvf[0, pl.ds(g * pieces, pieces)].reshape(all_rows, HD)
        values = with_ones(kvf[1, pl.ds(g * pieces, pieces)].reshape(all_rows, HD))
        for sub in range(0, group, SUB):
            scores = lax.dot_general(query_rows(g * group + sub), keys, dims, preferred_element_type=jnp.float32)
            part = pl.ds(sub * rows, SUB * rows)
            before = near_top[g, part]
            top = jnp.maximum(jnp.max(scores, axis=1, keepdims=True), before)
            wide_top = jnp.concatenate([top] * (all_rows // HD), axis=1)
            weights = jnp.exp2((scores - wide_top) * score_scale).astype(jnp.bfloat16)
            scale = jnp.exp2((before - top) * score_scale)
            summed = jnp.dot(weights, values, preferred_element_type=jnp.float32)
            summed += jnp.concatenate([scale, scale], axis=1) * near_sum[g, part]
            result = summed[:, :HD] / summed[:, HD:]
            for j in range(SUB):
                piece = jnp.where(live, result[j * rows : (j + 1) * rows], 0.0)
                out_ref[:, cols(g * group + sub + j)] = piece.astype(out_ref.dtype)

    reach = max(root_hops(root) + max(root, short - 1 - root) for root in roots)
    done = SIB + after(reach + z_hops)
    steps = SIB + after(reach + long - 1) + pairs

    def one_step(t, carry):
        @pl.when(t == 1)
        def _():
            wait_pages(1)

        @pl.when(t < pairs)
        def _():
            build(2 * t)
            build(2 * t + 1)
            sib_copy(t).start()

        @pl.when(t == SIB + 1)
        def _():
            for load in loads:
                load.wait()

        ahead = t - NEAR_STEP

        @pl.when((ahead >= 0) & (ahead < kv_heads))
        def _():
            near(ahead)

        gather(t)
        scan(t)
        spread(t)
        arrive(t)

        for n in range(3):
            @pl.when(t == PRE_STEPS[n])
            def _():
                pre_step(n)

        u = t - done

        @pl.when(at(u) & (lax.rem(u, per_head) == per_head - 1))
        def _():
            g = lax.div(u, per_head)
            attend(g)

        return carry

    lax.fori_loop(0, steps, one_step, 0)

    for d in range(1, short):
        pre_y(d, d).wait_send()
    for d in range(1, long):
        pre_z(d, d).wait_send()
    pre_sib(core).wait_send()
    half = pl.ds(0, pairs)
    every = pl.ds(0, chunks)
    remote(0, 0, 0, sib_s.at[every], sib_r.at[every], sibling).wait_send()
    for b, root in enumerate(roots):
        for kind, used in (
            (1, py < root),
            (2, py > root),
            (3, (py == root) & (pz < long - 1)),
            (4, (py == root) & (pz > 0)),
            (5, py >= 0),
            (6, (py >= root) & (py < short - 1)),
            (7, (py <= root) & (py > 0)),
        ):
            @pl.when(used)
            def _():
                remote(kind, b, 0, x.at[half], sib_r.at[half], sibling).wait_send()


def store(held_ref, out_hbm, sems):
    rows = held_ref.shape[0] // STORES
    copies = [
        pltpu.make_async_copy(held_ref.at[pl.ds(n * rows, rows)], out_hbm.at[pl.ds(n * rows, rows)], sems.at[n])
        for n in range(STORES)
    ]
    for copy in copies:
        copy.start()
    for copy in copies:
        copy.wait()


def solution(mesh):
    ring = mesh.shape["ctx"]

    def body(queries, new_keys, new_values, prefix_keys, prefix_values, pool_keys, pool_values, owners, lengths):
        heads = queries.shape[1] // HD
        kv_heads = new_keys.shape[1] // HD
        pages, page_rows = pool_keys.shape[1:3]
        pieces = pages * CUTS
        chunks = kv_heads * pieces
        c_rows = page_rows // CUTS
        long, short = grid_of(ring)
        chunk_buf = pltpu.VMEM((chunks, c_rows, HD), jnp.bfloat16)
        hbm = pl.BlockSpec(memory_space=pl.ANY)
        sm = pl.BlockSpec(memory_space=pltpu.SMEM)
        vmem = pl.BlockSpec(memory_space=pltpu.VMEM)
        held = pl.pallas_call(
            functools.partial(kernel, ring, heads, kv_heads),
            out_shape=pltpu.VMEM(queries.shape, jnp.bfloat16),
            in_specs=[hbm] * 7 + [sm] * 2,
            out_specs=vmem,
            scratch_shapes=[
                pltpu.VMEM((2, pages, page_rows, kv_heads * HD), jnp.bfloat16),
                pltpu.VMEM((2, long, short, 2) + prefix_keys.shape, jnp.bfloat16),
            ]
            + [chunk_buf] * 9
            + [
                pltpu.VMEM((2, chunks, c_rows, HD), jnp.bfloat16),
                pltpu.VMEM((queries.shape[0], queries.shape[0]), jnp.float32),
                pltpu.VMEM(queries.shape, jnp.bfloat16),
                pltpu.VMEM(new_keys.shape, jnp.bfloat16),
                pltpu.VMEM(new_values.shape, jnp.bfloat16),
                pltpu.VMEM((kv_heads, queries.shape[0] * heads // kv_heads, 2 * HD), jnp.float32),
                pltpu.VMEM((kv_heads, queries.shape[0] * heads // kv_heads, HD), jnp.float32),
                pltpu.SemaphoreType.DMA((2, 2)),
                pltpu.SemaphoreType.DMA((5,)),
                pltpu.SemaphoreType.DMA((short + long + 1,)),
                pltpu.SemaphoreType.DMA((short + long + 1,)),
                pltpu.SemaphoreType.DMA((8, 2)),
                pltpu.SemaphoreType.DMA((8, chunks)),
            ],
            compiler_params=pltpu.CompilerParams(
                collective_id=0, has_side_effects=True, vmem_limit_bytes=56 * 2**20
            ),
        )(queries, new_keys, new_values, prefix_keys, prefix_values, pool_keys, pool_values, owners, lengths)
        return pl.pallas_call(
            store,
            out_shape=jax.ShapeDtypeStruct(queries.shape, jnp.bfloat16),
            in_specs=[vmem],
            out_specs=hbm,
            scratch_shapes=[pltpu.SemaphoreType.DMA((STORES,))],
            compiler_params=pltpu.CompilerParams(vmem_limit_bytes=2**20),
        )(held)

    two = P(("groups", "ctx"), None)
    four = P(("groups", "ctx"), None, None, None)
    return jax.shard_map(
        body, mesh=mesh, in_specs=(two,) * 5 + (four,) * 2 + (P("groups"), P(("groups", "ctx"))),
        out_specs=two, check_vma=False,
    )
```

```python
import functools

import jax
import jax.numpy as jnp
from jax import lax
from jax.experimental import pallas as pl
from jax.experimental.pallas import tpu as pltpu
from jax.sharding import PartitionSpec as P

HD = 128
CUTS = 1
SIB = 1
HOP = (3, 1)
SUB = 2
SCORE_SCALE = 1.4426950408889634 / HD**0.5
DIMS = (((1,), (1,)), ((), ()))
PRE_STEPS = (2, 5, 6)
NEAR_STEP = 7
STORES = 4


def grid_of(ring):
    chips = ring // 2
    short = 1
    while (short * 2) ** 2 <= chips and chips % (short * 2) == 0:
        short *= 2
    return chips // short, short


def cols(g):
    return pl.ds(pl.multiple_of(g * HD, HD), HD)


def with_ones(values):
    return jnp.concatenate([values, jnp.ones_like(values)], axis=1)


def query_rows(q_ref, head):
    return jnp.concatenate([q_ref[:, cols(head + j)] for j in range(SUB)], axis=0)


def attend(g, kv_heads, length, q_ref, kvf, near_sum, near_top, out_ref, first):
    rows, group = q_ref.shape[0], q_ref.shape[1] // HD // kv_heads
    pieces = kvf.shape[1] // kv_heads
    all_rows = pieces * kvf.shape[2]
    live = lax.broadcasted_iota(jnp.int32, (rows, HD), 0) < length
    keys = kvf[0, pl.ds(g * pieces, pieces)].reshape(all_rows, HD)
    values = with_ones(kvf[1, pl.ds(g * pieces, pieces)].reshape(all_rows, HD))
    for sub in range(0, group, SUB):
        scores = lax.dot_general(query_rows(q_ref, g * group + sub), keys, DIMS, preferred_element_type=jnp.float32)
        part = pl.ds(sub * rows, SUB * rows)
        before = near_top[g, part]
        top = jnp.maximum(jnp.max(scores, axis=1, keepdims=True), before)
        wide_top = jnp.concatenate([top] * (all_rows // HD), axis=1)
        weights = jnp.exp2((scores - wide_top) * SCORE_SCALE).astype(jnp.bfloat16)
        scale = jnp.exp2((before - top) * SCORE_SCALE)
        summed = jnp.dot(weights, values, preferred_element_type=jnp.float32)
        summed += jnp.concatenate([scale, scale], axis=1) * near_sum[g, part]
        result = summed[:, :HD] / summed[:, HD:]
        for j in range(SUB):
            piece = jnp.where(live, result[j * rows : (j + 1) * rows], 0.0)
            out_ref[:, cols(first + sub + j)] = piece.astype(out_ref.dtype)


def kernel(
    ring, heads, kv_heads,
    q_hbm, nk_hbm, nv_hbm, pk_hbm, pv_hbm, poolk_hbm, poolv_hbm, owners_ref, lengths_ref,
    out_ref, kvf, q_ref, near_sum, near_top,
    page, pref, x, sib_s, sib_r, in_up, in_dn, up_s, up_r, dn_s, dn_r, bias, nk_ref, nv_ref,
    page_sems, load_sems, pre_send, pre_recv, send_sems, recv_sems,
):
    long, short = grid_of(ring)
    me = lax.axis_index("ctx")
    core = lax.rem(me, 2)
    chip = lax.div(me, 2)
    py = lax.rem(chip, short)
    pz = lax.div(chip, short)
    sibling = me + 1 - 2 * core
    sy, sz = 2, 2 * short

    barrier = pltpu.get_barrier_semaphore()

    def greet(target):
        pl.semaphore_signal(barrier, inc=1, device_id={"ctx": target})

    def y_peer(d):
        return me + (lax.rem(py + d, short) - py) * sy

    def z_peer(d):
        return me + (lax.rem(pz + d, long) - pz) * sz

    greet(sibling)
    for d in range(1, short):
        greet(y_peer(d))
    for d in range(1, long):
        greet(z_peer(d))
    peers = 1 + short - 1 + long - 1

    pages = poolk_hbm.shape[1]
    pieces = pages * CUTS
    page_rows = poolk_hbm.shape[2]
    blk = page_rows // CUTS
    chunks = kv_heads * pieces
    pairs = chunks // 2
    per_head = pieces // 2
    own_rows = pk_hbm.shape[0]
    pre = own_rows * ring
    rows = q_hbm.shape[0]
    group = heads // kv_heads
    width = kv_heads * HD

    splits = ((0, HD), (HD, width - HD))

    def page_copy(src, slot, part):
        start, size = splits[part]
        return pltpu.make_async_copy(
            src.at[0, :, :, pl.ds(start, size)], page.at[slot, :, :, pl.ds(start, size)], page_sems.at[slot, part]
        )

    def fetch(k_slot):
        for part in range(2):
            page_copy(poolk_hbm, k_slot, part).start()
            page_copy(poolv_hbm, 1 - k_slot, part).start()

    @pl.when(core == 0)
    def _():
        fetch(0)

    @pl.when(core == 1)
    def _():
        fetch(1)

    mine = pref.at[core, pz, py]
    own_pre = [pltpu.make_async_copy(src, mine.at[n], load_sems.at[n]) for n, src in enumerate((pk_hbm, pv_hbm))]
    for load in own_pre:
        load.start()

    loads = [
        pltpu.make_async_copy(src, dst, load_sems.at[n])
        for n, (src, dst) in enumerate(((q_hbm, q_ref), (nk_hbm, nk_ref), (nv_hbm, nv_ref)), start=2)
    ]
    for load in loads:
        load.start()

    length = lengths_ref[0]
    tok = lax.broadcasted_iota(jnp.int32, (rows, rows), 0)
    key = lax.broadcasted_iota(jnp.int32, (rows, rows), 1)
    bias[...] = jnp.where((key <= tok) & (key < length), 0.0, -1e30)

    def wait_pages(part):
        for slot in range(2):
            page_copy(poolk_hbm, slot, part).wait()

    def pre_y(d, source):
        return pltpu.make_async_remote_copy(
            src_ref=mine, dst_ref=mine, send_sem=pre_send.at[source], recv_sem=pre_recv.at[source],
            device_id={"ctx": y_peer(d)}, device_id_type=pl.DeviceIdType.MESH,
        )

    def pre_z(d, source):
        row = pref.at[core, pz]
        return pltpu.make_async_remote_copy(
            src_ref=row, dst_ref=row, send_sem=pre_send.at[short + source], recv_sem=pre_recv.at[short + source],
            device_id={"ctx": z_peer(d)}, device_id_type=pl.DeviceIdType.MESH,
        )

    def pre_sib(slot):
        return pltpu.make_async_remote_copy(
            src_ref=pref.at[slot], dst_ref=pref.at[slot], send_sem=pre_send.at[short + long], recv_sem=pre_recv.at[short + long],
            device_id={"ctx": sibling}, device_id_type=pl.DeviceIdType.MESH,
        )

    def pre_step(n):
        if n == 0:
            for d in range(1, short):
                pltpu.make_async_remote_copy(
                    src_ref=mine, dst_ref=pref.at[core, pz, lax.rem(py + short - d, short)], send_sem=pre_send.at[d],
                    recv_sem=pre_recv.at[d], device_id={"ctx": y_peer(d)}, device_id_type=pl.DeviceIdType.MESH,
                ).wait_recv()
            for d in range(1, long):
                pre_z(d, d).start()
        elif n == 1:
            for d in range(1, long):
                pltpu.make_async_remote_copy(
                    src_ref=pref.at[core, pz], dst_ref=pref.at[core, lax.rem(pz + long - d, long)], send_sem=pre_send.at[short + d],
                    recv_sem=pre_recv.at[short + d], device_id={"ctx": z_peer(d)}, device_id_type=pl.DeviceIdType.MESH,
                ).wait_recv()
            pre_sib(core).start()
        else:
            pre_sib(1 - core).wait_recv()

    for load in own_pre:
        load.wait()
    wait_pages(0)
    pl.semaphore_wait(barrier, peers)
    for d in range(1, short):
        pre_y(d, d).start()

    def remote(kind, b, i, src, dst, target):
        return pltpu.make_async_remote_copy(
            src_ref=src, dst_ref=dst, send_sem=send_sems.at[kind, b], recv_sem=recv_sems.at[kind, i],
            device_id={"ctx": target}, device_id_type=pl.DeviceIdType.MESH,
        )

    def build(i):
        g, b = lax.div(i, pieces), lax.rem(i, pieces)
        page_of = lax.div(b, CUTS)
        start = pl.multiple_of(lax.rem(b, CUTS) * blk, blk)
        held = jnp.where(owners_ref[page_of] == me, 1.0, 0.0).astype(jnp.float32)
        for slot, dst in ((1, sib_s), (0, x)):
            part = page[slot, page_of, pl.ds(start, blk), cols(g)]
            dst[i] = part * jnp.full(part.shape, held, jnp.float32).astype(jnp.bfloat16)

    def pair(u):
        return pl.ds(2 * u, 2)

    def sib_copy(u):
        return remote(0, 0, u, sib_s.at[pair(u)], sib_r.at[pair(u)], sibling)

    def in_up_copy(b, i):
        return remote(1, b, i, x.at[i], in_up.at[i], me + sy)

    def in_dn_copy(b, i):
        return remote(2, b, i, x.at[i], in_dn.at[i], me - sy)

    def up_copy(b, i, src):
        return remote(3, b, i, src.at[i], up_r.at[i], me + sz)

    def dn_copy(b, i, src):
        return remote(4, b, i, src.at[i], dn_r.at[i], me - sz)

    def share_copy(b, i):
        return remote(5, b, i, kvf.at[core, i], kvf.at[core, i], sibling)

    def out_up_copy(b, i):
        return remote(6, b, i, kvf.at[core, i], kvf.at[core, i], me + sy)

    def out_dn_copy(b, i):
        return remote(7, b, i, kvf.at[core, i], kvf.at[core, i], me - sy)

    depth = short // 2
    roots = (depth, depth - 1 + short % 2)

    def after(hops):
        return SIB + lax.div(hops * HOP[0], HOP[1]) if not isinstance(hops, int) else SIB + hops * HOP[0] // HOP[1]

    def at(u):
        return (u >= 0) & (u < pairs)

    def gather(t):
        u = t - SIB

        @pl.when(at(u))
        def _():
            sib_copy(u).wait_recv()
            x[pair(u)] = x[pair(u)] + sib_r[pair(u)]
            for b, root in enumerate(roots):
                if root > 0:
                    @pl.when(py == 0)
                    def _():
                        in_up_copy(b, 2 * u + b).start()

                if root < short - 1:
                    @pl.when(py == short - 1)
                    def _():
                        in_dn_copy(b, 2 * u + b).start()

        for b, root in enumerate(roots):
            for hop in range(1, root):
                up = t - after(hop)

                @pl.when(at(up) & (py == hop))
                def _():
                    i = 2 * up + b
                    in_up_copy(b, i).wait_recv()
                    x[i] = x[i] + in_up[i]
                    in_up_copy(b, i).start()

            for hop in range(1, short - 1 - root):
                dn = t - after(hop)

                @pl.when(at(dn) & (py == short - 1 - hop))
                def _():
                    i = 2 * dn + b
                    in_dn_copy(b, i).wait_recv()
                    x[i] = x[i] + in_dn[i]
                    in_dn_copy(b, i).start()

    def root_hops(root):
        return max(root, short - 1 - root)

    def scan(t):
        for b, root in enumerate(roots):
            hops = root_hops(root)
            r = t - after(hops)

            @pl.when(at(r) & (py == root))
            def _():
                i = 2 * r + b
                if root > 0:
                    in_up_copy(b, i).wait_recv()
                    x[i] = x[i] + in_up[i]
                if root < short - 1:
                    in_dn_copy(b, i).wait_recv()
                    x[i] = x[i] + in_dn[i]

                if long > 1:
                    @pl.when(pz == 0)
                    def _():
                        up_copy(b, i, x).start()

                    @pl.when(pz == long - 1)
                    def _():
                        dn_copy(b, i, x).start()

            up = t - after(hops + pz)

            @pl.when(at(up) & (py == root) & (pz > 0))
            def _():
                i = 2 * up + b
                up_copy(b, i, up_s).wait_recv()

                @pl.when(pz < long - 1)
                def _():
                    up_s[i] = x[i] + up_r[i]
                    up_copy(b, i, up_s).start()

            dn = t - after(hops + long - 1 - pz)

            @pl.when(at(dn) & (py == root) & (pz < long - 1))
            def _():
                i = 2 * dn + b
                dn_copy(b, i, dn_s).wait_recv()

                @pl.when(pz > 0)
                def _():
                    dn_s[i] = x[i] + dn_r[i]
                    dn_copy(b, i, dn_s).start()

    z_hops = jnp.maximum(pz, long - 1 - pz)

    def spread(t):
        for b, root in enumerate(roots):
            hops = root_hops(root) + z_hops
            end = t - after(hops)

            @pl.when(at(end) & (py == root))
            def _():
                i = 2 * end + b

                if long == 1:
                    kvf[core, i] = x[i]
                else:
                    @pl.when((pz > 0) & (pz < long - 1))
                    def _():
                        kvf[core, i] = x[i] + up_r[i] + dn_r[i]

                    @pl.when(pz == long - 1)
                    def _():
                        kvf[core, i] = x[i] + up_r[i]

                    @pl.when(pz == 0)
                    def _():
                        kvf[core, i] = x[i] + dn_r[i]

                if root < short - 1:
                    out_up_copy(b, i).start()
                if root > 0:
                    out_dn_copy(b, i).start()
                share_copy(b, i).start()

            above = jnp.where(py > root, py - root, root - py)
            out = t - after(hops + above)

            @pl.when(at(out) & (py > root))
            def _():
                i = 2 * out + b
                out_up_copy(b, i).wait_recv()

                @pl.when(py < short - 1)
                def _():
                    out_up_copy(b, i).start()

                share_copy(b, i).start()

            @pl.when(at(out) & (py < root))
            def _():
                i = 2 * out + b
                out_dn_copy(b, i).wait_recv()

                @pl.when(py > 0)
                def _():
                    out_dn_copy(b, i).start()

                share_copy(b, i).start()

    def far(root):
        return jnp.where(py > root, py - root, root - py)

    def arrive(t):
        for b, root in enumerate(roots):
            c = t - SIB - after(root_hops(root) + z_hops + far(root))

            @pl.when(at(c))
            def _():
                i = 2 * c + b
                remote(5, b, i, kvf.at[core, i], kvf.at[1 - core, i], sibling).wait_recv()

    def near(g):
        keys = jnp.concatenate([pref[:, :, :, 0, :, cols(g)].reshape(pre, HD), nk_ref[:, cols(g)]], axis=0)
        values = jnp.concatenate([pref[:, :, :, 1, :, cols(g)].reshape(pre, HD), nv_ref[:, cols(g)]], axis=0)
        values = with_ones(values)
        mask = jnp.concatenate([jnp.zeros((rows, pre), jnp.float32), bias[...]], axis=1)
        mask = jnp.concatenate([mask] * SUB, axis=0)
        for sub in range(0, group, SUB):
            scores = lax.dot_general(query_rows(q_ref, g * group + sub), keys, DIMS, preferred_element_type=jnp.float32) + mask
            top = jnp.max(scores, axis=1, keepdims=True)
            weights = jnp.exp2((scores - top) * SCORE_SCALE).astype(jnp.bfloat16)
            part = pl.ds(sub * rows, SUB * rows)
            near_sum[g, part] = jnp.dot(weights, values, preferred_element_type=jnp.float32)
            near_top[g, part] = jnp.broadcast_to(top, (SUB * rows, HD))

    reach = max(root_hops(root) + max(root, short - 1 - root) for root in roots)
    done = SIB + after(reach + z_hops)
    steps = SIB + after(reach + long - 1) + pairs

    def one_step(t, carry):
        @pl.when(t == 1)
        def _():
            wait_pages(1)

        @pl.when(t < pairs)
        def _():
            build(2 * t)
            build(2 * t + 1)
            sib_copy(t).start()

        @pl.when(t == SIB + 1)
        def _():
            for load in loads:
                load.wait()

        ahead = t - NEAR_STEP

        @pl.when((ahead >= 0) & (ahead < kv_heads))
        def _():
            near(ahead)

        gather(t)
        scan(t)
        spread(t)
        arrive(t)

        for n in range(3):
            @pl.when(t == PRE_STEPS[n])
            def _():
                pre_step(n)

        u = t - done

        @pl.when(at(u) & (lax.rem(u, per_head) == per_head - 1))
        def _():
            g = lax.div(u, per_head)

            @pl.when(g < kv_heads - 1)
            def _():
                attend(g, kv_heads, length, q_ref, kvf, near_sum, near_top, out_ref, g * group)

        return carry

    lax.fori_loop(0, steps, one_step, 0)

    for d in range(1, short):
        pre_y(d, d).wait_send()
    for d in range(1, long):
        pre_z(d, d).wait_send()
    pre_sib(core).wait_send()
    half = pl.ds(0, pairs)
    every = pl.ds(0, chunks)
    remote(0, 0, 0, sib_s.at[every], sib_r.at[every], sibling).wait_send()
    for b, root in enumerate(roots):
        for kind, used in (
            (1, py < root),
            (2, py > root),
            (3, (py == root) & (pz < long - 1)),
            (4, (py == root) & (pz > 0)),
            (5, py >= 0),
            (6, (py >= root) & (py < short - 1)),
            (7, (py <= root) & (py > 0)),
        ):
            @pl.when(used)
            def _():
                remote(kind, b, 0, x.at[half], sib_r.at[half], sibling).wait_send()


def finish(kv_heads, held_ref, kvf, q_ref, near_sum, near_top, lengths_ref, out_hbm, last_ref, sems):
    rows, width = held_ref.shape
    wide = width // kv_heads
    ready = pl.ds(0, width - wide)
    step = rows // STORES
    stores = [
        pltpu.make_async_copy(
            held_ref.at[pl.ds(n * step, step), ready], out_hbm.at[pl.ds(n * step, step), ready], sems.at[n]
        )
        for n in range(STORES)
    ]
    for store in stores:
        store.start()
    attend(kv_heads - 1, kv_heads, lengths_ref[0], q_ref, kvf, near_sum, near_top, last_ref, 0)
    last = pltpu.make_async_copy(last_ref, out_hbm.at[:, pl.ds(width - wide, wide)], sems.at[STORES])
    last.start()
    for store in stores:
        store.wait()
    last.wait()


def solution(mesh):
    ring = mesh.shape["ctx"]

    def body(queries, new_keys, new_values, prefix_keys, prefix_values, pool_keys, pool_values, owners, lengths):
        heads = queries.shape[1] // HD
        kv_heads = new_keys.shape[1] // HD
        pages, page_rows = pool_keys.shape[1:3]
        pieces = pages * CUTS
        chunks = kv_heads * pieces
        c_rows = page_rows // CUTS
        long, short = grid_of(ring)
        chunk_buf = pltpu.VMEM((chunks, c_rows, HD), jnp.bfloat16)
        hbm = pl.BlockSpec(memory_space=pl.ANY)
        sm = pl.BlockSpec(memory_space=pltpu.SMEM)
        vmem = pl.BlockSpec(memory_space=pltpu.VMEM)
        held = pl.pallas_call(
            functools.partial(kernel, ring, heads, kv_heads),
            out_shape=(
                pltpu.VMEM(queries.shape, jnp.bfloat16),
                pltpu.VMEM((2, chunks, c_rows, HD), jnp.bfloat16),
                pltpu.VMEM(queries.shape, jnp.bfloat16),
                pltpu.VMEM((kv_heads, queries.shape[0] * heads // kv_heads, 2 * HD), jnp.float32),
                pltpu.VMEM((kv_heads, queries.shape[0] * heads // kv_heads, HD), jnp.float32),
            ),
            in_specs=[hbm] * 7 + [sm] * 2,
            out_specs=(vmem,) * 5,
            scratch_shapes=[
                pltpu.VMEM((2, pages, page_rows, kv_heads * HD), jnp.bfloat16),
                pltpu.VMEM((2, long, short, 2) + prefix_keys.shape, jnp.bfloat16),
            ]
            + [chunk_buf] * 9
            + [
                pltpu.VMEM((queries.shape[0], queries.shape[0]), jnp.float32),
                pltpu.VMEM(new_keys.shape, jnp.bfloat16),
                pltpu.VMEM(new_values.shape, jnp.bfloat16),
                pltpu.SemaphoreType.DMA((2, 2)),
                pltpu.SemaphoreType.DMA((5,)),
                pltpu.SemaphoreType.DMA((short + long + 1,)),
                pltpu.SemaphoreType.DMA((short + long + 1,)),
                pltpu.SemaphoreType.DMA((8, 2)),
                pltpu.SemaphoreType.DMA((8, chunks)),
            ],
            compiler_params=pltpu.CompilerParams(
                collective_id=0, has_side_effects=True, vmem_limit_bytes=36 * 2**20
            ),
        )(queries, new_keys, new_values, prefix_keys, prefix_values, pool_keys, pool_values, owners, lengths)
        return pl.pallas_call(
            functools.partial(finish, kv_heads),
            out_shape=jax.ShapeDtypeStruct(queries.shape, jnp.bfloat16),
            in_specs=[vmem] * 5 + [sm],
            out_specs=hbm,
            scratch_shapes=[
                pltpu.VMEM((queries.shape[0], queries.shape[1] // kv_heads), jnp.bfloat16),
                pltpu.SemaphoreType.DMA((STORES + 1,)),
            ],
            compiler_params=pltpu.CompilerParams(vmem_limit_bytes=16 * 2**20),
        )(*held, lengths)

    two = P(("groups", "ctx"), None)
    four = P(("groups", "ctx"), None, None, None)
    return jax.shard_map(
        body, mesh=mesh, in_specs=(two,) * 5 + (four,) * 2 + (P("groups"), P(("groups", "ctx"))),
        out_specs=two, check_vma=False,
    )
```

```python
import functools

import jax
import jax.numpy as jnp
from jax import lax
from jax.experimental import pallas as pl
from jax.experimental.pallas import tpu as pltpu
from jax.sharding import PartitionSpec as P

HD = 128
CUTS = 1
SIB = 1
HOP = (3, 1)
SUB = 2
SCORE_SCALE = 1.4426950408889634 / HD**0.5
DIMS = (((1,), (1,)), ((), ()))
PRE_STEPS = (2, 5, 6)
NEAR_STEP = 7
STORES = 4


def grid_of(ring):
    chips = ring // 2
    short = 1
    while (short * 2) ** 2 <= chips and chips % (short * 2) == 0:
        short *= 2
    return chips // short, short


def cols(g):
    return pl.ds(pl.multiple_of(g * HD, HD), HD)


def with_ones(values):
    return jnp.concatenate([values, jnp.ones_like(values)], axis=1)


def query_rows(q_ref, head):
    return jnp.concatenate([q_ref[:, cols(head + j)] for j in range(SUB)], axis=0)


def attend(g, kv_heads, length, q_ref, kvf, near_sum, near_top, out_ref, first):
    rows, group = q_ref.shape[0], q_ref.shape[1] // HD // kv_heads
    pieces = kvf.shape[1] // kv_heads
    all_rows = pieces * kvf.shape[2]
    live = lax.broadcasted_iota(jnp.int32, (rows, HD), 0) < length
    keys = kvf[0, pl.ds(g * pieces, pieces)].reshape(all_rows, HD)
    values = with_ones(kvf[1, pl.ds(g * pieces, pieces)].reshape(all_rows, HD))
    for sub in range(0, group, SUB):
        scores = lax.dot_general(query_rows(q_ref, g * group + sub), keys, DIMS, preferred_element_type=jnp.float32)
        part = pl.ds(sub * rows, SUB * rows)
        before = near_top[g, part]
        top = jnp.maximum(jnp.max(scores, axis=1, keepdims=True), before)
        wide_top = jnp.concatenate([top] * (all_rows // HD), axis=1)
        weights = jnp.exp2((scores - wide_top) * SCORE_SCALE).astype(jnp.bfloat16)
        scale = jnp.exp2((before - top) * SCORE_SCALE)
        summed = jnp.dot(weights, values, preferred_element_type=jnp.float32)
        summed += jnp.concatenate([scale, scale], axis=1) * near_sum[g, part]
        result = summed[:, :HD] / summed[:, HD:]
        for j in range(SUB):
            piece = jnp.where(live, result[j * rows : (j + 1) * rows], 0.0)
            out_ref[:, cols(first + sub + j)] = piece.astype(out_ref.dtype)


def kernel(
    ring, heads, kv_heads,
    q_hbm, nk_hbm, nv_hbm, pk_hbm, pv_hbm, poolk_hbm, poolv_hbm, owners_ref, lengths_ref,
    out_ref, kvf, q_ref, near_sum, near_top,
    page, pref, x, sib_s, sib_r, in_up, in_dn, up_s, up_r, dn_s, dn_r, bias, nk_ref, nv_ref,
    page_sems, load_sems, pre_send, pre_recv, send_sems, recv_sems,
):
    long, short = grid_of(ring)
    me = lax.axis_index("ctx")
    core = lax.rem(me, 2)
    chip = lax.div(me, 2)
    py = lax.rem(chip, short)
    pz = lax.div(chip, short)
    sibling = me + 1 - 2 * core
    sy, sz = 2, 2 * short

    barrier = pltpu.get_barrier_semaphore()

    def greet(target):
        pl.semaphore_signal(barrier, inc=1, device_id={"ctx": target})

    def y_peer(d):
        return me + (lax.rem(py + d, short) - py) * sy

    def z_peer(d):
        return me + (lax.rem(pz + d, long) - pz) * sz

    greet(sibling)
    for d in range(1, short):
        greet(y_peer(d))
    for d in range(1, long):
        greet(z_peer(d))
    peers = 1 + short - 1 + long - 1

    pages = poolk_hbm.shape[1]
    pieces = pages * CUTS
    page_rows = poolk_hbm.shape[2]
    blk = page_rows // CUTS
    chunks = kv_heads * pieces
    pairs = chunks // 2
    per_head = pieces // 2
    own_rows = pk_hbm.shape[0]
    pre = own_rows * ring
    rows = q_hbm.shape[0]
    group = heads // kv_heads
    width = kv_heads * HD

    splits = ((0, HD), (HD, width - HD))

    def page_copy(src, slot, part):
        start, size = splits[part]
        return pltpu.make_async_copy(
            src.at[0, :, :, pl.ds(start, size)], page.at[slot, :, :, pl.ds(start, size)], page_sems.at[slot, part]
        )

    def fetch(k_slot):
        for part in range(2):
            page_copy(poolk_hbm, k_slot, part).start()
            page_copy(poolv_hbm, 1 - k_slot, part).start()

    @pl.when(core == 0)
    def _():
        fetch(0)

    @pl.when(core == 1)
    def _():
        fetch(1)

    mine = pref.at[core, pz, py]
    own_pre = [pltpu.make_async_copy(src, mine.at[n], load_sems.at[n]) for n, src in enumerate((pk_hbm, pv_hbm))]
    for load in own_pre:
        load.start()

    loads = [
        pltpu.make_async_copy(src, dst, load_sems.at[n])
        for n, (src, dst) in enumerate(((q_hbm, q_ref), (nk_hbm, nk_ref), (nv_hbm, nv_ref)), start=2)
    ]
    for load in loads:
        load.start()

    length = lengths_ref[0]
    tok = lax.broadcasted_iota(jnp.int32, (rows, rows), 0)
    key = lax.broadcasted_iota(jnp.int32, (rows, rows), 1)
    bias[...] = jnp.where((key <= tok) & (key < length), 0.0, -1e30)

    def wait_pages(part):
        for slot in range(2):
            page_copy(poolk_hbm, slot, part).wait()

    def pre_copy(n, src, dst, target):
        return pltpu.make_async_remote_copy(
            src_ref=src, dst_ref=dst, send_sem=pre_send.at[n], recv_sem=pre_recv.at[n],
            device_id={"ctx": target}, device_id_type=pl.DeviceIdType.MESH,
        )

    def y_from(d):
        return lax.rem(py + short - d, short)

    def z_from(d):
        return lax.rem(pz + long - d, long)

    def pre_y(d):
        return pre_copy(d, mine, mine, y_peer(d))

    def pre_z(d):
        return pre_copy(short + d, mine, mine, z_peer(d))

    def pre_on(d, e):
        block = pref.at[core, pz, y_from(e)]
        return pre_copy(short + long + d * short + e, block, block, z_peer(d))

    def pre_sib(slot):
        return pre_copy(0, pref.at[slot], pref.at[slot], sibling)

    def pre_step(n):
        if n == 0:
            for e in range(1, short):
                pre_copy(e, mine, pref.at[core, pz, y_from(e)], y_peer(e)).wait_recv()
            for d in range(1, long):
                for e in range(1, short):
                    pre_on(d, e).start()
        elif n == 1:
            for d in range(1, long):
                pre_copy(short + d, mine, pref.at[core, z_from(d), py], z_peer(d)).wait_recv()
                for e in range(1, short):
                    n = short + long + d * short + e
                    pre_copy(n, mine, pref.at[core, z_from(d), y_from(e)], z_peer(d)).wait_recv()
            pre_sib(core).start()
        else:
            pre_sib(1 - core).wait_recv()

    for load in own_pre:
        load.wait()
    pl.semaphore_wait(barrier, peers)
    for d in range(1, short):
        pre_y(d).start()
    for d in range(1, long):
        pre_z(d).start()
    wait_pages(0)

    def remote(kind, b, i, src, dst, target):
        return pltpu.make_async_remote_copy(
            src_ref=src, dst_ref=dst, send_sem=send_sems.at[kind, b], recv_sem=recv_sems.at[kind, i],
            device_id={"ctx": target}, device_id_type=pl.DeviceIdType.MESH,
        )

    def build(i):
        g, b = lax.div(i, pieces), lax.rem(i, pieces)
        page_of = lax.div(b, CUTS)
        start = pl.multiple_of(lax.rem(b, CUTS) * blk, blk)
        held = jnp.where(owners_ref[page_of] == me, 1.0, 0.0).astype(jnp.float32)
        for slot, dst in ((1, sib_s), (0, x)):
            part = page[slot, page_of, pl.ds(start, blk), cols(g)]
            dst[i] = part * jnp.full(part.shape, held, jnp.float32).astype(jnp.bfloat16)

    def pair(u):
        return pl.ds(2 * u, 2)

    def sib_copy(u):
        return remote(0, 0, u, sib_s.at[pair(u)], sib_r.at[pair(u)], sibling)

    def in_up_copy(b, i):
        return remote(1, b, i, x.at[i], in_up.at[i], me + sy)

    def in_dn_copy(b, i):
        return remote(2, b, i, x.at[i], in_dn.at[i], me - sy)

    def up_copy(b, i, src):
        return remote(3, b, i, src.at[i], up_r.at[i], me + sz)

    def dn_copy(b, i, src):
        return remote(4, b, i, src.at[i], dn_r.at[i], me - sz)

    def share_copy(b, i):
        return remote(5, b, i, kvf.at[core, i], kvf.at[core, i], sibling)

    def out_up_copy(b, i):
        return remote(6, b, i, kvf.at[core, i], kvf.at[core, i], me + sy)

    def out_dn_copy(b, i):
        return remote(7, b, i, kvf.at[core, i], kvf.at[core, i], me - sy)

    depth = short // 2
    roots = (depth, depth - 1 + short % 2)

    def after(hops):
        return SIB + lax.div(hops * HOP[0], HOP[1]) if not isinstance(hops, int) else SIB + hops * HOP[0] // HOP[1]

    def at(u):
        return (u >= 0) & (u < pairs)

    def gather(t):
        u = t - SIB

        @pl.when(at(u))
        def _():
            sib_copy(u).wait_recv()
            x[pair(u)] = x[pair(u)] + sib_r[pair(u)]
            for b, root in enumerate(roots):
                if root > 0:
                    @pl.when(py == 0)
                    def _():
                        in_up_copy(b, 2 * u + b).start()

                if root < short - 1:
                    @pl.when(py == short - 1)
                    def _():
                        in_dn_copy(b, 2 * u + b).start()

        for b, root in enumerate(roots):
            for hop in range(1, root):
                up = t - after(hop)

                @pl.when(at(up) & (py == hop))
                def _():
                    i = 2 * up + b
                    in_up_copy(b, i).wait_recv()
                    x[i] = x[i] + in_up[i]
                    in_up_copy(b, i).start()

            for hop in range(1, short - 1 - root):
                dn = t - after(hop)

                @pl.when(at(dn) & (py == short - 1 - hop))
                def _():
                    i = 2 * dn + b
                    in_dn_copy(b, i).wait_recv()
                    x[i] = x[i] + in_dn[i]
                    in_dn_copy(b, i).start()

    def root_hops(root):
        return max(root, short - 1 - root)

    def scan(t):
        for b, root in enumerate(roots):
            hops = root_hops(root)
            r = t - after(hops)

            @pl.when(at(r) & (py == root))
            def _():
                i = 2 * r + b
                if root > 0:
                    in_up_copy(b, i).wait_recv()
                    x[i] = x[i] + in_up[i]
                if root < short - 1:
                    in_dn_copy(b, i).wait_recv()
                    x[i] = x[i] + in_dn[i]

                if long > 1:
                    @pl.when(pz == 0)
                    def _():
                        up_copy(b, i, x).start()

                    @pl.when(pz == long - 1)
                    def _():
                        dn_copy(b, i, x).start()

            up = t - after(hops + pz)

            @pl.when(at(up) & (py == root) & (pz > 0))
            def _():
                i = 2 * up + b
                up_copy(b, i, up_s).wait_recv()

                @pl.when(pz < long - 1)
                def _():
                    up_s[i] = x[i] + up_r[i]
                    up_copy(b, i, up_s).start()

            dn = t - after(hops + long - 1 - pz)

            @pl.when(at(dn) & (py == root) & (pz < long - 1))
            def _():
                i = 2 * dn + b
                dn_copy(b, i, dn_s).wait_recv()

                @pl.when(pz > 0)
                def _():
                    dn_s[i] = x[i] + dn_r[i]
                    dn_copy(b, i, dn_s).start()

    z_hops = jnp.maximum(pz, long - 1 - pz)

    def spread(t):
        for b, root in enumerate(roots):
            hops = root_hops(root) + z_hops
            end = t - after(hops)

            @pl.when(at(end) & (py == root))
            def _():
                i = 2 * end + b

                if long == 1:
                    kvf[core, i] = x[i]
                else:
                    @pl.when((pz > 0) & (pz < long - 1))
                    def _():
                        kvf[core, i] = x[i] + up_r[i] + dn_r[i]

                    @pl.when(pz == long - 1)
                    def _():
                        kvf[core, i] = x[i] + up_r[i]

                    @pl.when(pz == 0)
                    def _():
                        kvf[core, i] = x[i] + dn_r[i]

                if root < short - 1:
                    out_up_copy(b, i).start()
                if root > 0:
                    out_dn_copy(b, i).start()
                share_copy(b, i).start()

            above = jnp.where(py > root, py - root, root - py)
            out = t - after(hops + above)

            @pl.when(at(out) & (py > root))
            def _():
                i = 2 * out + b
                out_up_copy(b, i).wait_recv()

                @pl.when(py < short - 1)
                def _():
                    out_up_copy(b, i).start()

                share_copy(b, i).start()

            @pl.when(at(out) & (py < root))
            def _():
                i = 2 * out + b
                out_dn_copy(b, i).wait_recv()

                @pl.when(py > 0)
                def _():
                    out_dn_copy(b, i).start()

                share_copy(b, i).start()

    def far(root):
        return jnp.where(py > root, py - root, root - py)

    def arrive(t):
        for b, root in enumerate(roots):
            c = t - SIB - after(root_hops(root) + z_hops + far(root))

            @pl.when(at(c))
            def _():
                i = 2 * c + b
                remote(5, b, i, kvf.at[core, i], kvf.at[1 - core, i], sibling).wait_recv()

    def near(g):
        keys = jnp.concatenate([pref[:, :, :, 0, :, cols(g)].reshape(pre, HD), nk_ref[:, cols(g)]], axis=0)
        values = jnp.concatenate([pref[:, :, :, 1, :, cols(g)].reshape(pre, HD), nv_ref[:, cols(g)]], axis=0)
        values = with_ones(values)
        mask = jnp.concatenate([jnp.zeros((rows, pre), jnp.float32), bias[...]], axis=1)
        mask = jnp.concatenate([mask] * SUB, axis=0)
        for sub in range(0, group, SUB):
            scores = lax.dot_general(query_rows(q_ref, g * group + sub), keys, DIMS, preferred_element_type=jnp.float32) + mask
            top = jnp.max(scores, axis=1, keepdims=True)
            weights = jnp.exp2((scores - top) * SCORE_SCALE).astype(jnp.bfloat16)
            part = pl.ds(sub * rows, SUB * rows)
            near_sum[g, part] = jnp.dot(weights, values, preferred_element_type=jnp.float32)
            near_top[g, part] = jnp.broadcast_to(top, (SUB * rows, HD))

    reach = max(root_hops(root) + max(root, short - 1 - root) for root in roots)
    done = SIB + after(reach + z_hops)
    steps = SIB + after(reach + long - 1) + pairs

    def one_step(t, carry):
        @pl.when(t == 1)
        def _():
            wait_pages(1)

        @pl.when(t < pairs)
        def _():
            build(2 * t)
            build(2 * t + 1)
            sib_copy(t).start()

        @pl.when(t == SIB + 1)
        def _():
            for load in loads:
                load.wait()

        ahead = t - NEAR_STEP

        @pl.when((ahead >= 0) & (ahead < kv_heads))
        def _():
            near(ahead)

        gather(t)
        scan(t)
        spread(t)
        arrive(t)

        for n in range(3):
            @pl.when(t == PRE_STEPS[n])
            def _():
                pre_step(n)

        u = t - done

        @pl.when(at(u) & (lax.rem(u, per_head) == per_head - 1))
        def _():
            g = lax.div(u, per_head)

            @pl.when(g < kv_heads - 1)
            def _():
                attend(g, kv_heads, length, q_ref, kvf, near_sum, near_top, out_ref, g * group)

        return carry

    lax.fori_loop(0, steps, one_step, 0)

    for d in range(1, short):
        pre_y(d).wait_send()
    for d in range(1, long):
        pre_z(d).wait_send()
        for e in range(1, short):
            pre_on(d, e).wait_send()
    pre_sib(core).wait_send()
    half = pl.ds(0, pairs)
    every = pl.ds(0, chunks)
    remote(0, 0, 0, sib_s.at[every], sib_r.at[every], sibling).wait_send()
    for b, root in enumerate(roots):
        for kind, used in (
            (1, py < root),
            (2, py > root),
            (3, (py == root) & (pz < long - 1)),
            (4, (py == root) & (pz > 0)),
            (5, py >= 0),
            (6, (py >= root) & (py < short - 1)),
            (7, (py <= root) & (py > 0)),
        ):
            @pl.when(used)
            def _():
                remote(kind, b, 0, x.at[half], sib_r.at[half], sibling).wait_send()


def finish(kv_heads, held_ref, kvf, q_ref, near_sum, near_top, lengths_ref, out_hbm, last_ref, sems):
    rows, width = held_ref.shape
    wide = width // kv_heads
    ready = pl.ds(0, width - wide)
    step = rows // STORES
    stores = [
        pltpu.make_async_copy(
            held_ref.at[pl.ds(n * step, step), ready], out_hbm.at[pl.ds(n * step, step), ready], sems.at[n]
        )
        for n in range(STORES)
    ]
    for store in stores:
        store.start()
    attend(kv_heads - 1, kv_heads, lengths_ref[0], q_ref, kvf, near_sum, near_top, last_ref, 0)
    last = pltpu.make_async_copy(last_ref, out_hbm.at[:, pl.ds(width - wide, wide)], sems.at[STORES])
    last.start()
    for store in stores:
        store.wait()
    last.wait()


def solution(mesh):
    ring = mesh.shape["ctx"]

    def body(queries, new_keys, new_values, prefix_keys, prefix_values, pool_keys, pool_values, owners, lengths):
        heads = queries.shape[1] // HD
        kv_heads = new_keys.shape[1] // HD
        pages, page_rows = pool_keys.shape[1:3]
        pieces = pages * CUTS
        chunks = kv_heads * pieces
        c_rows = page_rows // CUTS
        long, short = grid_of(ring)
        chunk_buf = pltpu.VMEM((chunks, c_rows, HD), jnp.bfloat16)
        hbm = pl.BlockSpec(memory_space=pl.ANY)
        sm = pl.BlockSpec(memory_space=pltpu.SMEM)
        vmem = pl.BlockSpec(memory_space=pltpu.VMEM)
        held = pl.pallas_call(
            functools.partial(kernel, ring, heads, kv_heads),
            out_shape=(
                pltpu.VMEM(queries.shape, jnp.bfloat16),
                pltpu.VMEM((2, chunks, c_rows, HD), jnp.bfloat16),
                pltpu.VMEM(queries.shape, jnp.bfloat16),
                pltpu.VMEM((kv_heads, queries.shape[0] * heads // kv_heads, 2 * HD), jnp.float32),
                pltpu.VMEM((kv_heads, queries.shape[0] * heads // kv_heads, HD), jnp.float32),
            ),
            in_specs=[hbm] * 7 + [sm] * 2,
            out_specs=(vmem,) * 5,
            scratch_shapes=[
                pltpu.VMEM((2, pages, page_rows, kv_heads * HD), jnp.bfloat16),
                pltpu.VMEM((2, long, short, 2) + prefix_keys.shape, jnp.bfloat16),
            ]
            + [chunk_buf] * 9
            + [
                pltpu.VMEM((queries.shape[0], queries.shape[0]), jnp.float32),
                pltpu.VMEM(new_keys.shape, jnp.bfloat16),
                pltpu.VMEM(new_values.shape, jnp.bfloat16),
                pltpu.SemaphoreType.DMA((2, 2)),
                pltpu.SemaphoreType.DMA((5,)),
                pltpu.SemaphoreType.DMA((short + long + long * short,)),
                pltpu.SemaphoreType.DMA((short + long + long * short,)),
                pltpu.SemaphoreType.DMA((8, 2)),
                pltpu.SemaphoreType.DMA((8, chunks)),
            ],
            compiler_params=pltpu.CompilerParams(
                collective_id=0, has_side_effects=True, vmem_limit_bytes=36 * 2**20
            ),
        )(queries, new_keys, new_values, prefix_keys, prefix_values, pool_keys, pool_values, owners, lengths)
        return pl.pallas_call(
            functools.partial(finish, kv_heads),
            out_shape=jax.ShapeDtypeStruct(queries.shape, jnp.bfloat16),
            in_specs=[vmem] * 5 + [sm],
            out_specs=hbm,
            scratch_shapes=[
                pltpu.VMEM((queries.shape[0], queries.shape[1] // kv_heads), jnp.bfloat16),
                pltpu.SemaphoreType.DMA((STORES + 1,)),
            ],
            compiler_params=pltpu.CompilerParams(vmem_limit_bytes=16 * 2**20),
        )(*held, lengths)

    two = P(("groups", "ctx"), None)
    four = P(("groups", "ctx"), None, None, None)
    return jax.shard_map(
        body, mesh=mesh, in_specs=(two,) * 5 + (four,) * 2 + (P("groups"), P(("groups", "ctx"))),
        out_specs=two, check_vma=False,
    )
```
